256 devices in a mesh: ctx: 64 (over z, y, core), head: 4 (over x).
Axes of the slice: x: 4, y: 4, z: 8, core: 2. Of those that a mesh axis runs over, the one named last changes fastest.
Arguments:
- queries: bfloat16 [8192, 4096], P('ctx', 'head'), may hold values from -12 to 12
- keys: bfloat16 [8192, 512], P('ctx', 'head'), may hold values from -6 to 6
- values: bfloat16 [8192, 512], P('ctx', 'head'), may hold values from -18 to 18
- doc_ids: int32 [8192], P('ctx'), may hold values from 0 to 15, never falling along the last dimension, each value on 1 to 6144 neighbouring positions
- plan: int32 [64, 64], P('ctx'), may hold values from 0 to 63, each once within a row
- w_out: bfloat16 [4096, 8192], P('head', 'ctx'), may hold values from -0.09375 to 0.09375
Outputs:
- output: bfloat16 [8192, 8192], P('ctx', 'head')
The draws below stay inside these ranges and needn't reach their ends.
Inputs may be any that keep to these rules, and one draw needn't show every extreme that they name: doc_ids never fall along the window; every one of the 16 documents holds 1 to 6144 positions, and one holds exactly 6144. Each row of plan is a permutation of the device indices along ctx.
All inputs are finite; a program needn't handle non-finite values.
Results may differ from the reference program's by a relative error of at most 0.01.
Values may be sent and summed in bfloat16 or wider, within the bound.
A program may use at most 64 MiB of HBM per device.

```python
import math
import jax
import jax.numpy as jnp
import numpy as np
from jax import lax

TOK_DEV = 128
HEADS = 32
KV_HEADS = 4
HEAD_DIM = 128
D = 8192
DOCS = 16
TOKENS = 8192
PIECE = 2
MAXDOC = 6144
N_CTX = 64
N_HEAD = 4


def draw_queries(key, part):
    main_key = jax.random.fold_in(key, 1)
    result = jnp.clip(2.0 * jax.random.normal(main_key, (TOKENS, HEADS * HEAD_DIM), jnp.float32), -12.0, 12.0)
    return result.astype(jnp.bfloat16)


def draw_keys(key, part):
    main_key = jax.random.fold_in(key, 2)
    result = jnp.clip(jax.random.normal(main_key, (TOKENS, KV_HEADS * HEAD_DIM), jnp.float32), -6.0, 6.0)
    return result.astype(jnp.bfloat16)


def level_of(stream_key, dims, shards, low, largest):
    factor_of = 1.0
    for position, shards_of in shards:
        draws = jax.random.uniform(jax.random.fold_in(jax.random.fold_in(stream_key, 6), position), (shards_of,), jnp.float32, low / len(shards), largest / len(shards))
        factor_of = factor_of * jnp.repeat(jnp.exp(draws), dims[position] // shards_of).reshape((-1,) + (1,) * (len(dims) - 1 - position))
    return factor_of


def length_profile(number_of, total, most, skew):
    portions = [(1 << 20) // math.isqrt(standing ** skew) + 1 for standing in range(2, number_of + 1)]
    surplus, counts = total - most - (number_of - 1), [1] * (number_of - 1)
    while surplus > 0:
        free = [i for i in range(number_of - 1) if counts[i] < most]
        whole, left = sum([portions[i] for i in free]), surplus
        for i in free:
            more = min(most - counts[i], max(1, left * portions[i] // whole), surplus)
            counts[i] = counts[i] + more
            surplus = surplus - more
    return np.array([most] + counts)


def uneven(stream_key, number_of, total, reach, slope):
    if number_of == 2:
        one = jax.random.randint(stream_key, (), max(1, total - reach), min(reach, total - 1) + 1)
        return jnp.stack([one, total - one])
    lengths = jnp.asarray(length_profile(number_of, total, reach, slope), jnp.int32)
    twos = (number_of - 1) // 2
    giver, sink = lengths[1:1 + 2 * twos:2], lengths[2:2 + 2 * twos:2]
    margin = jnp.minimum(giver - 1, reach - sink)
    moved = jax.random.randint(jax.random.fold_in(stream_key, 1), (twos,), 0, 1 << 20) % (margin + 1)
    lengths = lengths.at[1:1 + 2 * twos:2].set(giver - moved).at[2:2 + 2 * twos:2].set(sink + moved)
    return lengths[jax.random.permutation(jax.random.fold_in(stream_key, 2), number_of)]


def gaussian(rng, dims, scale, bound, cuts=(), kind=jnp.bfloat16):
    drawn = scale * jax.random.normal(rng, dims, jnp.float32)
    if cuts:
        drawn = drawn * level_of(rng, dims, cuts, -0.22, 0.18)
    return jnp.clip(drawn, -bound, bound).astype(kind)


def setup_inputs(seed: int = 0) -> dict:
    key_of = jax.random.split(jax.random.key(seed), 7)
    return {
        "queries": draw_queries(jax.random.fold_in(key_of[6], 71), 0),
        "keys": draw_keys(jax.random.fold_in(key_of[6], 71), 0),
        "values": gaussian(key_of[2], (TOKENS, KV_HEADS * HEAD_DIM), 3.0, 18.0, ((0, 64), (1, 4))),
        "doc_ids": jnp.searchsorted(jnp.cumsum(uneven(key_of[3], DOCS, TOKENS, MAXDOC, 2)), jnp.arange(TOKENS), side="right").astype(jnp.int32),
        "plan": jax.vmap(lambda own: jax.random.permutation(own, N_CTX))(jax.random.split(key_of[4], N_CTX)).reshape((N_CTX, N_CTX)).astype(jnp.int32),
        "w_out": gaussian(key_of[5], (HEADS * HEAD_DIM, D), (HEADS * HEAD_DIM) ** -0.5, 0.09375, ((0, 4), (1, 64))),
    }


NEG_FILL = -1e+30

def head_attention(operands, allowed, score_scale):
    query_head, key_head, value_head = operands
    scores = jnp.einsum('bgd,ld->gbl', query_head.astype(jnp.float32), key_head.astype(jnp.float32)) * score_scale
    scores = jnp.where(allowed[None], scores, NEG_FILL)
    row_max = lax.optimization_barrier(jnp.max(scores, axis=-1, keepdims=True))
    expo = jnp.where(allowed[None], jnp.exp(scores - row_max), 0.0)
    totals = lax.optimization_barrier(jnp.sum(expo, axis=-1))
    rounded = lax.optimization_barrier(expo.astype(jnp.bfloat16)).astype(jnp.float32)
    numer = jnp.einsum('gbl,ld->gbd', rounded, value_head.astype(jnp.float32))
    return numer / totals[..., None]

def reference(queries, keys, values, doc_ids, plan, w_out):
    doc_range = jnp.arange(DOCS, dtype=jnp.int32)
    doc_first = lax.optimization_barrier(jnp.sum((doc_ids[None, :] < doc_range[:, None]).astype(jnp.int32), axis=1))
    doc_start = doc_first[doc_ids]
    group_size = HEADS // KV_HEADS
    score_scale = 1.0 / math.sqrt(HEAD_DIM)
    q_all = queries.reshape(TOKENS, KV_HEADS, group_size, HEAD_DIM).transpose(1, 0, 2, 3)
    k_all = keys.reshape(TOKENS, KV_HEADS, HEAD_DIM).transpose(1, 0, 2)
    v_all = values.reshape(TOKENS, KV_HEADS, HEAD_DIM).transpose(1, 0, 2)
    block_size = min(512, TOKENS)
    results = []
    for block_index in range(TOKENS // block_size):
        lower = block_index * block_size
        upper = lower + block_size
        row_pos = jnp.arange(lower, upper, dtype=jnp.int32)
        row_start = doc_start[lower:upper]
        key_pos = jnp.arange(upper, dtype=jnp.int32)
        allowed = (key_pos[None, :] >= row_start[:, None]) & (key_pos[None, :] <= row_pos[:, None])
        per_head = lax.map(partial_head(allowed, score_scale), (q_all[:, lower:upper], k_all[:, :upper], v_all[:, :upper]))
        block_out = per_head.transpose(2, 0, 1, 3).reshape(block_size, HEADS * HEAD_DIM)
        results.append(block_out.astype(jnp.bfloat16))
    attended = jnp.concatenate(results, axis=0)
    slot_index = jnp.arange(N_CTX, dtype=jnp.int32)
    within = jnp.arange(PIECE, dtype=jnp.int32)
    source_pos = slot_index[None, :, None] * TOK_DEV + plan.T[:, :, None] * PIECE + within[None, None, :]
    arranged = attended[source_pos.reshape(-1).astype(jnp.int32)]
    rows_per = HEADS * HEAD_DIM // N_HEAD
    summed = jnp.zeros((TOKENS, D), jnp.float32)
    for group_index in range(N_HEAD):
        lower = group_index * rows_per
        upper = lower + rows_per
        partial_sum = jnp.dot(arranged[:, lower:upper], w_out[lower:upper], preferred_element_type=jnp.float32)
        summed = summed + lax.optimization_barrier(partial_sum.astype(jnp.bfloat16)).astype(jnp.float32)
    return summed.astype(jnp.bfloat16)

def partial_head(allowed, score_scale):

    def run_head(operands):
        return head_attention(operands, allowed, score_scale)
    return run_head
```

```python
import functools
import math

import jax
import jax.numpy as jnp
from jax import lax
from jax.experimental import pallas as pl
from jax.experimental.pallas import tpu as pltpu
from jax.sharding import PartitionSpec as P

HEAD_DIM = 128
DOCS = 16
NEG_FILL = -1e30


def attend_kernel(T, TK, q_ref, meta_ref, ids_ref, kv_ref, o_ref):
    ids = ids_ref[...]
    local = meta_ref[:, 0:1]
    doc = meta_ref[:, 1:2]
    n_tok = q_ref.shape[0]
    G = q_ref.shape[1] // HEAD_DIM
    start = jnp.zeros_like(doc)
    for d in range(1, DOCS):
        first = jnp.sum(jnp.where(ids < d, 1.0, 0.0))
        start = jnp.where(doc == d, first, start)
    slot = lax.broadcasted_iota(jnp.int32, (n_tok, 1), 0) // 2
    pos = local + 128.0 * slot.astype(jnp.float32)
    c = math.log2(math.e) / math.sqrt(HEAD_DIM)
    KB = TK // 128
    for b in range(n_tok // T):
        rows = pl.ds(b * T, T)
        st = start[b * T : (b + 1) * T]
        po = pos[b * T : (b + 1) * T]
        q = jnp.concatenate(
            [q_ref[rows, h * HEAD_DIM : (h + 1) * HEAD_DIM] for h in range(G)], axis=0
        )
        lo = jnp.min(st).astype(jnp.int32) // TK
        hi = jnp.max(po).astype(jnp.int32) // TK + 1

        def step(j, carry):
            m, l, acc = carry
            k = kv_ref[pl.ds(j * KB, KB), 0:128, 0:128].reshape(TK, HEAD_DIM)
            v = kv_ref[pl.ds(j * KB, KB), 0:128, 128:256].reshape(TK, HEAD_DIM)
            s = lax.dot_general(
                q, k, (((1,), (1,)), ((), ())), preferred_element_type=jnp.float32
            )
            u = (j * TK + lax.broadcasted_iota(jnp.int32, (T, TK), 1)).astype(jnp.float32)
            ok = (u >= st) & (u <= po)
            s = jnp.where(ok[None], s.reshape(G, T, TK), NEG_FILL).reshape(G * T, TK)
            m_new = jnp.maximum(m, jnp.max(s, axis=1, keepdims=True))
            p = jnp.exp2((s - m_new) * c)
            a = jnp.exp2((m - m_new) * c)
            part = p[:, 0:128]
            for i in range(1, KB):
                part = part + p[:, i * 128 : (i + 1) * 128]
            l = l * a + part
            acc = acc * a + jnp.dot(
                p.astype(jnp.bfloat16), v, preferred_element_type=jnp.float32
            )
            return m_new, l, acc

        R = G * T
        m, l, acc = lax.fori_loop(
            lo,
            hi,
            step,
            (
                jnp.full((R, 1), NEG_FILL, jnp.float32),
                jnp.zeros((R, 128), jnp.float32),
                jnp.zeros((R, HEAD_DIM), jnp.float32),
            ),
        )
        out = (acc / jnp.sum(l, axis=1, keepdims=True)).astype(jnp.bfloat16)
        for h in range(G):
            o_ref[rows, h * HEAD_DIM : (h + 1) * HEAD_DIM] = out[h * T : (h + 1) * T]


def attend(q, meta, ids, kv, T=32, TK=1024):
    vm = pl.BlockSpec(memory_space=pltpu.VMEM)
    return pl.pallas_call(
        functools.partial(attend_kernel, T, TK),
        out_shape=jax.ShapeDtypeStruct(q.shape, jnp.bfloat16),
        in_specs=[vm] * 4,
        out_specs=vm,
        compiler_params=pltpu.CompilerParams(vmem_limit_bytes=40 << 20),
    )(q, meta, ids, kv)


def body(queries, keys, values, doc_ids, plan, w_out):
    n_rows, width = queries.shape
    parts = lax.axis_size("ctx")
    piece = n_rows // parts
    id_rows = jnp.pad(
        doc_ids.astype(jnp.bfloat16)[None, :], ((0, 15), (0, 256 - n_rows))
    )
    kv = jnp.concatenate([jnp.concatenate([keys, values], axis=1), id_rows], axis=0)
    all_kv = lax.all_gather(kv, "ctx", axis=0, tiled=False)
    w_all = lax.all_gather(w_out, "ctx", axis=1, tiled=True)
    local = jnp.arange(n_rows, dtype=jnp.int32).astype(jnp.bfloat16)
    extra = jnp.pad(
        jnp.stack([local, doc_ids.astype(jnp.bfloat16)], axis=1), ((0, 0), (0, 126))
    )
    rows = jnp.concatenate([queries, extra], axis=1).reshape(parts, piece, width + 128)
    rows = jnp.take(rows, plan[0], axis=0, mode="clip")
    moved = lax.all_to_all(rows, "ctx", split_axis=0, concat_axis=0, tiled=True)
    moved = moved.reshape(n_rows, width + 128)
    attended = attend(
        moved[:, :width],
        moved[:, width : width + 2].astype(jnp.float32),
        all_kv[:, n_rows, :n_rows].astype(jnp.float32),
        all_kv,
    )
    partial_sum = jnp.dot(attended, w_all, preferred_element_type=jnp.float32)
    return lax.psum_scatter(
        partial_sum.astype(jnp.bfloat16), "head", scatter_dimension=1, tiled=True
    )


def solution(mesh):
    return jax.shard_map(
        body,
        mesh=mesh,
        in_specs=(
            P("ctx", "head"),
            P("ctx", "head"),
            P("ctx", "head"),
            P("ctx"),
            P("ctx", None),
            P("head", "ctx"),
        ),
        out_specs=P("ctx", "head"),
        check_vma=False,
    )
```

```python
import functools
import math

import jax
import jax.numpy as jnp
from jax import lax
from jax.experimental import pallas as pl
from jax.experimental.pallas import tpu as pltpu
from jax.sharding import Mesh, PartitionSpec as P

HEAD_DIM = 128
DOCS = 16
NEG_FILL = -1e30

MESH = pl.DeviceIdType.MESH
STEPS = (0, -1, 1, -2, 2, -3, 3, 4)


def remote(src, dst, send, recv, **where):
    return pltpu.make_async_remote_copy(
        src_ref=src, dst_ref=dst, send_sem=send, recv_sem=recv,
        device_id=where, device_id_type=MESH)


def project_kernel(a_ref, w_ref, o_ref, A, W, PB, RO, RA, FB,
                   sa, ra, ss, rs, sw, rw, sx, rx, sr, rr, so, ro, lo):
    z, y, k, x = (lax.axis_index(n) for n in ("z", "y", "core", "head"))
    zn, yn, xn = 8, 4, 4
    zp, zm = (z + 1) % zn, (z + zn - 1) % zn
    yp, ym, y2 = (y + 1) % yn, (y + yn - 1) % yn, (y + 2) % yn
    xp, xm = (x + 1) % xn, (x + xn - 1) % xn
    sib = 1 - k
    T = a_ref.shape[0]
    half = T // 2
    KD = w_ref.shape[0]

    barrier = pltpu.get_barrier_semaphore()
    others = [(dy, dk) for dy in range(4) for dk in range(2) if (dy, dk) != (0, 0)]
    for where in [{"z": zp}, {"z": zm}, {"head": xp}, {"head": xm}] + [
        {"y": (y + dy) % yn, "core": (k + dk) % 2} for dy, dk in others]:
        pl.semaphore_signal(barrier, inc=1, device_id=where, device_id_type=MESH)
    pl.semaphore_wait(barrier, 4 + len(others))

    def aslot(yy, kk):
        return A.at[yy * 2 + kk]

    own_a = pltpu.make_async_copy(a_ref, aslot(y, k), lo.at[0])
    own_w = pltpu.make_async_copy(w_ref, W.at[z], lo.at[1])
    a_out = [
        remote(a_ref, aslot(y, k), sa.at[0], ra.at[0], y=yp),
        remote(a_ref, aslot(y, k), sa.at[1], ra.at[1], y=ym),
        remote(aslot(ym, k).at[0:half], aslot(ym, k).at[0:half], sa.at[2], ra.at[2], y=yp),
        remote(aslot(yp, k).at[half:T], aslot(yp, k).at[half:T], sa.at[3], ra.at[3], y=ym),
    ]
    a_in = [
        remote(a_ref, aslot(ym, k), sa.at[0], ra.at[0], y=yp),
        remote(a_ref, aslot(yp, k), sa.at[1], ra.at[1], y=ym),
        remote(aslot(y2, k).at[0:half], aslot(y2, k).at[0:half], sa.at[2], ra.at[2], y=yp),
        remote(aslot(y2, k).at[half:T], aslot(y2, k).at[half:T], sa.at[3], ra.at[3], y=ym),
    ]
    s_out = [remote(a_ref, aslot(y, k), ss.at[0], rs.at[0], core=sib)] + [
        remote(aslot(yy, k), aslot(yy, k), ss.at[i], rs.at[i], core=sib)
        for i, yy in ((1, ym), (2, yp), (3, y2))]
    s_in = [
        remote(aslot(yy, sib), aslot(yy, sib), ss.at[i], rs.at[i], core=sib)
        for i, yy in ((0, y), (1, ym), (2, yp), (3, y2))]
    zs = [(z + d + zn) % zn for d in STEPS]
    kh = KD // 2

    def wcopy(i, src_slot, lo_, hi_, to, first=None):
        src = W.at[src_slot].at[lo_:hi_] if first is None else first
        return remote(src, W.at[src_slot].at[lo_:hi_], sw.at[i], rw.at[i], z=to)

    w_out = [
        wcopy(0, z, 0, KD, zp, w_ref), wcopy(1, z, 0, KD, zm, w_ref),
        wcopy(2, zs[1], 0, KD, zp), wcopy(3, zs[2], 0, KD, zm),
        wcopy(4, zs[3], 0, KD, zp), wcopy(5, zs[4], 0, KD, zm),
        wcopy(6, zs[5], 0, kh, zp), wcopy(7, zs[6], kh, KD, zm),
    ]
    w_in = [
        wcopy(0, zs[1], 0, KD, zp), wcopy(1, zs[2], 0, KD, zm),
        wcopy(2, zs[3], 0, KD, zp), wcopy(3, zs[4], 0, KD, zm),
        wcopy(4, zs[5], 0, KD, zp), wcopy(5, zs[6], 0, KD, zm),
        wcopy(6, zs[7], 0, kh, zp), wcopy(7, zs[7], kh, KD, zm),
    ]
    a_out[0].start()
    a_out[1].start()
    w_out[0].start()
    w_out[1].start()
    s_out[0].start()
    own_a.start()
    own_w.start()
    a_in[0].wait_recv()
    a_out[2].start()
    a_in[1].wait_recv()
    a_out[3].start()
    s_out[1].start()
    s_out[2].start()
    w_in[0].wait_recv()
    w_out[2].start()
    w_in[1].wait_recv()
    w_out[3].start()
    a_in[2].wait_recv()
    a_in[3].wait_recv()
    s_out[3].start()
    own_a.wait()
    own_w.wait()
    for c in s_in:
        c.wait_recv()

    delta = [((zi // 2) + xn - x) % xn for zi in zs]
    par = [zi % 2 for zi in zs]

    def to_adjacent(src, p):
        return remote(src, RO.at[p], sx.at[p], rx.at[p], head=xp if p == 0 else xm)

    def to_dest(src, side, p):
        return remote(src, RA.at[side, p], sr.at[side, p], rr.at[side, p], head=xp if side == 0 else xm)

    def compute(s):
        w = W.at[zs[s]]

        @pl.loop(0, 4)
        def _(i):
            rows = A[pl.ds(i * 2, 2)].reshape(2 * T, KD)
            res = jnp.dot(rows, w[...], preferred_element_type=jnp.float32)
            PB[s, pl.ds(i * 2, 2)] = res.astype(jnp.bfloat16).reshape(2, T, 128)

        for p in (0, 1):
            @pl.when(jnp.logical_and(delta[s] == 2, par[s] == p))
            def _():
                to_adjacent(PB.at[s], p).start()
        @pl.when(jnp.logical_and(delta[s] == 1, par[s] == 1))
        def _():
            to_dest(PB.at[s], 0, 1).start()
        @pl.when(jnp.logical_and(delta[s] == 3, par[s] == 0))
        def _():
            to_dest(PB.at[s], 1, 0).start()

    def middle(s):
        for side, p in ((0, 0), (1, 1)):
            @pl.when(jnp.logical_and(delta[s] == (1 if side == 0 else 3), par[s] == p))
            def _():
                to_adjacent(PB.at[s], p).wait_recv()
                PB[s] = (PB[s].astype(jnp.float32) + RO[p].astype(jnp.float32)).astype(jnp.bfloat16)
                to_dest(PB.at[s], side, p).start()

    def back(p, dy, dk, src):
        yy, kk = (y + dy) % yn, (k + dk) % 2
        col = pl.multiple_of((p * 8 + y * 2 + k) * 128, 128)
        return remote(FB.at[p, yy * 2 + kk], o_ref.at[:, pl.ds(col, 128)],
                      so.at[p, dy * 2 + dk], ro.at[p, dy * 2 + dk], y=yy, core=kk)

    def back_in(p, dy, dk):
        yy, kk = (y + yn - dy) % yn, (k + 2 - dk) % 2
        col = pl.multiple_of((p * 8 + yy * 2 + kk) * 128, 128)
        return remote(FB.at[p, 0], o_ref.at[:, pl.ds(col, 128)],
                      so.at[p, dy * 2 + dk], ro.at[p, dy * 2 + dk], y=y2)

    def own_back(p):
        col = pl.multiple_of((p * 8 + y * 2 + k) * 128, 128)
        return pltpu.make_async_copy(FB.at[p, y * 2 + k], o_ref.at[:, pl.ds(col, 128)], lo.at[2 + p])

    def last(s):
        for p in (0, 1):
            @pl.when(jnp.logical_and(delta[s] == 0, par[s] == p))
            def _():
                to_dest(PB.at[s], 0, p).wait_recv()
                to_dest(PB.at[s], 1, p).wait_recv()
                FB[p] = (PB[s].astype(jnp.float32) + RA[0, p].astype(jnp.float32)
                         + RA[1, p].astype(jnp.float32)).astype(jnp.bfloat16)
                for dy, dk in others:
                    back(p, dy, dk, None).start()
                own_back(p).start()

    L1, L2 = 1, 3
    for s in range(8 + L2):
        if s < 8:
            if s == 7:
                w_in[6].wait_recv()
                w_in[7].wait_recv()
            elif s >= 3:
                w_in[s - 1].wait_recv()
                w_out[s + 1].start()
            compute(s)
        if L1 <= s < 8 + L1:
            middle(s - L1)
        if L2 <= s:
            last(s - L2)
    for p in (0, 1):
        for dy, dk in others:
            back_in(p, dy, dk).wait_recv()
        own_back(p).wait()
    for c in a_out + s_out + w_out:
        c.wait_send()
    for p in (0, 1):
        to_adjacent(PB.at[0], p).wait_send()
        for side in (0, 1):
            to_dest(PB.at[0], side, p).wait_send()
        for dy, dk in others:
            back(p, dy, dk, None).wait_send()


def project(attended, w_out, cid=1):
    T, KD = attended.shape
    any_ = pl.BlockSpec(memory_space=pl.ANY)
    dma = pltpu.SemaphoreType.DMA
    bf = jnp.bfloat16
    return pl.pallas_call(
        project_kernel,
        out_shape=jax.ShapeDtypeStruct((T, 2048), bf),
        in_specs=[any_, any_], out_specs=any_,
        scratch_shapes=[
            pltpu.VMEM((8, T, KD), bf), pltpu.VMEM((8, KD, 128), bf), pltpu.VMEM((8, 8, T, 128), bf),
            pltpu.VMEM((2, 8, T, 128), bf), pltpu.VMEM((2, 2, 8, T, 128), bf), pltpu.VMEM((2, 8, T, 128), bf),
            dma((4,)), dma((4,)), dma((4,)), dma((4,)), dma((8,)), dma((8,)),
            dma((2,)), dma((2,)), dma((2, 2)), dma((2, 2)), dma((2, 8)), dma((2, 8)), dma((4,)),
        ],
        compiler_params=pltpu.CompilerParams(collective_id=cid, has_side_effects=True, vmem_limit_bytes=40 << 20),
    )(attended, w_out)


def gather_kernel(kv_ref, o_ref, sz, rz, sy, ry, sy2, ry2, ss, rs, lo):
    z, y, k, x = (lax.axis_index(n) for n in ("z", "y", "core", "head"))
    zn, yn = 8, 4
    zp, zm = (z + 1) % zn, (z + zn - 1) % zn
    yp, ym, y2 = (y + 1) % yn, (y + yn - 1) % yn, (y + 2) % yn
    sib = 1 - k
    N = kv_ref.shape[0]
    H = 128
    barrier = pltpu.get_barrier_semaphore()
    for where in [{"z": zp}, {"z": zm}, {"y": yp}, {"y": ym}, {"core": sib}]:
        pl.semaphore_signal(barrier, inc=1, device_id=where, device_id_type=MESH)
    pl.semaphore_wait(barrier, 5)
    zs = [(z + d + zn) % zn for d in STEPS]

    def slot(zz, yy, kk):
        return o_ref.at[(zz * yn + yy) * 2 + kk]

    def zc(i, zz, a, b, to, src=None):
        d = slot(zz, y, k).at[a:b]
        return remote(d if src is None else src, d, sz.at[i], rz.at[i], z=to)

    z_out = [zc(0, z, 0, N, zp, kv_ref), zc(1, z, 0, N, zm, kv_ref),
             zc(2, zs[1], 0, N, zp), zc(3, zs[2], 0, N, zm),
             zc(4, zs[3], 0, N, zp), zc(5, zs[4], 0, N, zm),
             zc(6, zs[5], 0, H, zp), zc(7, zs[6], H, N, zm)]
    z_in = [zc(0, zs[1], 0, N, zp), zc(1, zs[2], 0, N, zm),
            zc(2, zs[3], 0, N, zp), zc(3, zs[4], 0, N, zm),
            zc(4, zs[5], 0, N, zp), zc(5, zs[6], 0, N, zm),
            zc(6, zs[7], 0, H, zp), zc(7, zs[7], H, N, zm)]

    def yc(s, side, yy, src=None):
        d = slot(zs[s], yy, k)
        return remote(d if src is None else src, d, sy.at[s, side], ry.at[s, side], y=yp if side == 0 else ym)

    def yc2(s, side, yy):
        d = slot(zs[s], yy, k)
        d = d.at[0:H] if side == 0 else d.at[H:N]
        return remote(d, d, sy2.at[s, side], ry2.at[s, side], y=yp if side == 0 else ym)

    ys = (y, ym, yp, y2)

    def sc(s, i, kk, src=None):
        d = slot(zs[s], ys[i], kk)
        return remote(d if src is None else src, d, ss.at[s, i], rs.at[s, i], core=sib)

    own = pltpu.make_async_copy(kv_ref, slot(z, y, k), lo.at[0])

    def zstage(s):
        src = kv_ref if s == 0 else None
        if s == 0:
            z_out[0].start()
            z_out[1].start()
            own.start()
        elif s == 7:
            z_in[6].wait_recv()
            z_in[7].wait_recv()
        else:
            z_in[s - 1].wait_recv()
            z_out[s + 1].start()
        yc(s, 0, y, src).start()
        yc(s, 1, y, src).start()
        sc(s, 0, k, src).start()

    def y1stage(s):
        yc(s, 0, ym).wait_recv()
        yc2(s, 0, ym).start()
        sc(s, 1, k).start()
        yc(s, 1, yp).wait_recv()
        yc2(s, 1, yp).start()
        sc(s, 2, k).start()

    def y2stage(s):
        yc2(s, 0, y2).wait_recv()
        yc2(s, 1, y2).wait_recv()
        sc(s, 3, k).start()

    for s in range(10):
        if s < 8:
            zstage(s)
        if 1 <= s < 9:
            y1stage(s - 1)
        if 2 <= s:
            y2stage(s - 2)
    own.wait()
    for s in range(8):
        for i in range(4):
            sc(s, i, sib).wait_recv()
    for s in range(8):
        z_out[s].wait_send()
        yc(s, 0, y).wait_send()
        yc(s, 1, y).wait_send()
        yc2(s, 0, ym).wait_send()
        yc2(s, 1, yp).wait_send()
        for i in range(4):
            sc(s, i, k).wait_send()


def gather(kv, cid=0):
    N = kv.shape[0]
    any_ = pl.BlockSpec(memory_space=pl.ANY)
    dma = pltpu.SemaphoreType.DMA
    return pl.pallas_call(
        gather_kernel,
        out_shape=jax.ShapeDtypeStruct((64, N, 128), kv.dtype),
        in_specs=[any_], out_specs=any_,
        scratch_shapes=[dma((8,)), dma((8,)), dma((8, 2)), dma((8, 2)), dma((8, 2)), dma((8, 2)),
                        dma((8, 4)), dma((8, 4)), dma((1,))],
        compiler_params=pltpu.CompilerParams(collective_id=cid, has_side_effects=True),
    )(kv)


def attend_kernel(T, TK, q_ref, meta_ref, ids_ref, kv_ref, o_ref):
    ids = ids_ref[...]
    local = meta_ref[:, 0:1]
    doc = meta_ref[:, 1:2]
    n_tok = q_ref.shape[0]
    G = q_ref.shape[1] // HEAD_DIM
    start = jnp.zeros_like(doc)
    for d in range(1, DOCS):
        first = jnp.sum(jnp.where(ids < d, 1.0, 0.0))
        start = jnp.where(doc == d, first, start)
    slot = lax.broadcasted_iota(jnp.int32, (n_tok, 1), 0) // 2
    pos = local + 128.0 * slot.astype(jnp.float32)
    c = math.log2(math.e) / math.sqrt(HEAD_DIM)
    KB = TK // 128
    for b in range(n_tok // T):
        rows = pl.ds(b * T, T)
        st = start[b * T : (b + 1) * T]
        po = pos[b * T : (b + 1) * T]
        q = jnp.concatenate(
            [q_ref[rows, h * HEAD_DIM : (h + 1) * HEAD_DIM] for h in range(G)], axis=0
        )
        lo = jnp.min(st).astype(jnp.int32) // TK
        hi = jnp.max(po).astype(jnp.int32) // TK + 1

        def step(j, carry):
            m, l, acc = carry
            k = kv_ref[pl.ds(j * KB, KB), 0:128, :].reshape(TK, HEAD_DIM)
            v = kv_ref[pl.ds(j * KB, KB), 128:256, :].reshape(TK, HEAD_DIM)
            s = lax.dot_general(
                q, k, (((1,), (1,)), ((), ())), preferred_element_type=jnp.float32
            )
            u = (j * TK + lax.broadcasted_iota(jnp.int32, (T, TK), 1)).astype(jnp.float32)
            ok = (u >= st) & (u <= po)
            s = jnp.where(ok[None], s.reshape(G, T, TK), NEG_FILL).reshape(G * T, TK)
            m_new = jnp.maximum(m, jnp.max(s, axis=1, keepdims=True))
            p = jnp.exp2((s - m_new) * c)
            a = jnp.exp2((m - m_new) * c)
            part = p[:, 0:128]
            for i in range(1, KB):
                part = part + p[:, i * 128 : (i + 1) * 128]
            l = l * a + part
            acc = acc * a + jnp.dot(
                p.astype(jnp.bfloat16), v, preferred_element_type=jnp.float32
            )
            return m_new, l, acc

        R = G * T
        m, l, acc = lax.fori_loop(
            lo,
            hi,
            step,
            (
                jnp.full((R, 1), NEG_FILL, jnp.float32),
                jnp.zeros((R, 128), jnp.float32),
                jnp.zeros((R, HEAD_DIM), jnp.float32),
            ),
        )
        out = (acc / jnp.sum(l, axis=1, keepdims=True)).astype(jnp.bfloat16)
        for h in range(G):
            o_ref[rows, h * HEAD_DIM : (h + 1) * HEAD_DIM] = out[h * T : (h + 1) * T]


def attend(q, meta, ids, kv, T=32, TK=1024):
    vm = pl.BlockSpec(memory_space=pltpu.VMEM)
    return pl.pallas_call(
        functools.partial(attend_kernel, T, TK),
        out_shape=jax.ShapeDtypeStruct(q.shape, jnp.bfloat16),
        in_specs=[vm] * 4,
        out_specs=vm,
        compiler_params=pltpu.CompilerParams(vmem_limit_bytes=40 << 20),
    )(q, meta, ids, kv)


CTX = ("z", "y", "core")


def body(queries, keys, values, doc_ids, plan, w_out):
    n_rows, width = queries.shape
    parts = 64
    piece = n_rows // parts
    id_rows = jnp.pad(doc_ids.astype(jnp.bfloat16)[None, :], ((0, 15), (0, 0)))
    kv = jnp.concatenate([keys, values, id_rows], axis=0)
    local = jnp.arange(n_rows, dtype=jnp.int32).astype(jnp.bfloat16)
    extra = jnp.pad(
        jnp.stack([local, doc_ids.astype(jnp.bfloat16)], axis=1), ((0, 0), (0, 126))
    )
    rows = jnp.concatenate([queries, extra], axis=1).reshape(parts, piece, width + 128)
    rows = jnp.take(rows, plan[0], axis=0, mode="clip")
    moved = lax.all_to_all(rows, CTX, split_axis=0, concat_axis=0, tiled=True)
    moved = moved.reshape(n_rows, width + 128)
    all_kv = gather(kv)
    attended = attend(
        moved[:, :width],
        moved[:, width : width + 2].astype(jnp.float32),
        all_kv[:, 256, :].astype(jnp.float32),
        all_kv,
    )
    return project(attended, w_out)


def solution(mesh):
    fine = Mesh(mesh.devices.reshape(8, 4, 2, 4), CTX + ("head",))
    return jax.shard_map(
        body,
        mesh=fine,
        in_specs=(
            P(CTX, "head"),
            P(CTX, "head"),
            P(CTX, "head"),
            P(CTX),
            P(CTX, None),
            P("head", CTX),
        ),
        out_specs=P(CTX, "head"),
        check_vma=False,
    )
```

```python
import functools
import math

import jax
import jax.numpy as jnp
from jax import lax
from jax.experimental import pallas as pl
from jax.experimental.pallas import tpu as pltpu
from jax.sharding import Mesh, PartitionSpec as P

HEAD_DIM = 128
NEG_FILL = -1e30

MESH = pl.DeviceIdType.MESH
STEPS = (0, -1, 1, -2, 2, -3, 3, 4)
ZN, YN, XN = 8, 4, 4


def remote(src, dst, send, recv, **where):
    return pltpu.make_async_remote_copy(
        src_ref=src, dst_ref=dst, send_sem=send, recv_sem=recv,
        device_id=where, device_id_type=MESH)


def layer_kernel(T, q_ref, meta_ref, kv_ref, w_ref, o_ref,
                 KV, A, W, PB, RO, RA, FB, M, L, ACC,
                 sz, rz, sy, ry, sy2, ry2, ss, rs, sw, rw,
                 sa, ra, sh, rh, sas, ras, sx, rx, sr, rr, so, ro, lo):
    z, y, k, x = (lax.axis_index(n) for n in ("z", "y", "core", "head"))
    zp, zm = (z + 1) % ZN, (z + ZN - 1) % ZN
    yp, ym, y2 = (y + 1) % YN, (y + YN - 1) % YN, (y + 2) % YN
    xp, xm = (x + 1) % XN, (x + XN - 1) % XN
    sib = 1 - k
    NT = q_ref.shape[0]
    G = q_ref.shape[1] // HEAD_DIM
    N = kv_ref.shape[0]
    KD = w_ref.shape[0]
    H, HT, HK = 128, NT // 2, KD // 2
    zs = [(z + d + ZN) % ZN for d in STEPS]
    ys = (y, ym, yp, y2)

    barrier = pltpu.get_barrier_semaphore()
    group = [(dy, dk) for dy in range(YN) for dk in range(2) if (dy, dk) != (0, 0)]
    for where in [{"z": zp}, {"z": zm}, {"head": xp}, {"head": xm}] + [
        {"y": (y + dy) % YN, "core": (k + dk) % 2} for dy, dk in group]:
        pl.semaphore_signal(barrier, inc=1, device_id=where, device_id_type=MESH)
    pl.semaphore_wait(barrier, 4 + len(group))

    def slot(zz, yy, kk):
        return KV.at[(zz * YN + yy) * 2 + kk]

    def zc(i, zz, a, b, to, src=None):
        d = slot(zz, y, k).at[a:b]
        return remote(d if src is None else src, d, sz.at[i], rz.at[i], z=to)

    z_out = [zc(0, z, 0, N, zp, kv_ref), zc(1, z, 0, N, zm, kv_ref),
             zc(2, zs[1], 0, N, zp), zc(3, zs[2], 0, N, zm),
             zc(4, zs[3], 0, N, zp), zc(5, zs[4], 0, N, zm),
             zc(6, zs[5], 0, H, zp), zc(7, zs[6], H, N, zm)]
    z_in = [zc(0, zs[1], 0, N, zp), zc(1, zs[2], 0, N, zm),
            zc(2, zs[3], 0, N, zp), zc(3, zs[4], 0, N, zm),
            zc(4, zs[5], 0, N, zp), zc(5, zs[6], 0, N, zm),
            zc(6, zs[7], 0, H, zp), zc(7, zs[7], H, N, zm)]

    def yc(s, side, yy, src=None):
        d = slot(zs[s], yy, k)
        return remote(d if src is None else src, d, sy.at[s, side], ry.at[s, side], y=yp if side == 0 else ym)

    def yc2(s, side, yy):
        d = slot(zs[s], yy, k)
        d = d.at[0:H] if side == 0 else d.at[H:N]
        return remote(d, d, sy2.at[s, side], ry2.at[s, side], y=yp if side == 0 else ym)

    def sc(s, i, kk, src=None):
        d = slot(zs[s], ys[i], kk)
        return remote(d if src is None else src, d, ss.at[s, i], rs.at[s, i], core=sib)

    own_kv = pltpu.make_async_copy(kv_ref, slot(z, y, k), lo.at[0])

    def wc(dist, side, h, src_z, src=None):
        d = W.at[src_z].at[h * HK:(h + 1) * HK]
        return remote(d if src is None else src, d, sw.at[dist - 1, side, h], rw.at[dist - 1, side, h],
                      z=zp if side == 0 else zm)

    def zat(side, dist):
        return (z + (ZN - dist if side == 0 else dist)) % ZN

    own_w = pltpu.make_async_copy(w_ref, W.at[z], lo.at[1])

    def wstart():
        for h in (0, 1):
            for side in (0, 1):
                wc(1, side, h, z, w_ref.at[h * HK:(h + 1) * HK]).start()
        own_w.start()

    def wevent(dist, h):
        for side in (0, 1):
            if dist == 4 and side != h:
                continue
            src = zat(side, dist)
            wc(dist, side, h, src).wait_recv()
            if dist < 3 or (dist == 3 and side == h):
                wc(dist + 1, side, h, src).start()

    w_events = [(d, h) for d in (1, 2, 3, 4) for h in (0, 1)]

    def zstage(s):
        src = kv_ref if s == 0 else None
        if s == 0:
            z_out[0].start()
            z_out[1].start()
        elif s == 7:
            z_in[6].wait_recv()
            z_in[7].wait_recv()
        else:
            z_in[s - 1].wait_recv()
            z_out[s + 1].start()
        yc(s, 0, y, src).start()
        yc(s, 1, y, src).start()
        sc(s, 0, k, src).start()
        if s == 0:
            own_kv.start()
            wstart()

    def y1stage(s):
        yc(s, 0, ym).wait_recv()
        yc2(s, 0, ym).start()
        sc(s, 1, k).start()
        yc(s, 1, yp).wait_recv()
        yc2(s, 1, yp).start()
        sc(s, 2, k).start()

    def y2stage(s):
        yc2(s, 0, y2).wait_recv()
        yc2(s, 1, y2).wait_recv()
        sc(s, 3, k).start()

    B = NT // T
    R = G * T
    TK = 2 * YN * 128
    c = math.log2(math.e) / math.sqrt(HEAD_DIM)
    M[...] = jnp.full_like(M, NEG_FILL)
    L[...] = jnp.zeros_like(L)
    ACC[...] = jnp.zeros_like(ACC)

    def attention(s):
        if s == 0:
            own_kv.wait()
        for i in range(4):
            sc(s, i, sib).wait_recv()
        zz = zs[s]
        base = zz * 2 * YN

        def unit(b, carry):
            rows = pl.ds(pl.multiple_of(b * T, T), T)
            q = jnp.concatenate([q_ref[rows, h * HEAD_DIM:(h + 1) * HEAD_DIM] for h in range(G)], axis=0)
            pos, doc = meta_ref[rows, 0:1], meta_ref[rows, 1:2]
            kk = KV[pl.ds(base, 2 * YN), 0:128, :].reshape(TK, HEAD_DIM)
            vv = KV[pl.ds(base, 2 * YN), 128:256, :].reshape(TK, HEAD_DIM)
            ids = jnp.concatenate([KV[base + i, 256:272, :].astype(jnp.float32)[0:1] for i in range(2 * YN)], axis=1)
            u = (zz * TK + lax.broadcasted_iota(jnp.int32, (T, TK), 1)).astype(jnp.float32)
            ok = (ids == doc) & (u <= pos)
            sco = lax.dot_general(q, kk, (((1,), (1,)), ((), ())), preferred_element_type=jnp.float32)
            sco = jnp.where(ok[None], sco.reshape(G, T, TK), NEG_FILL).reshape(R, TK)
            m = M[b][:, 0:1]
            m_new = jnp.maximum(m, jnp.max(sco, axis=1, keepdims=True))
            p = jnp.exp2((sco - m_new) * c)
            a = jnp.exp2((m - m_new) * c)
            part = p[:, 0:128]
            for i in range(1, TK // 128):
                part = part + p[:, i * 128:(i + 1) * 128]
            L[b] = L[b] * a + part
            ACC[b] = ACC[b] * a + jnp.dot(p.astype(jnp.bfloat16), vv, preferred_element_type=jnp.float32)
            M[b] = jnp.broadcast_to(m_new, (R, 128))
            return carry

        per = T * 64 // TK
        lax.fori_loop(zz // per, B, unit, 0)

    LAG = 3
    for i in range(8 + LAG):
        if i < 8:
            zstage(i)
        if 1 <= i < 9:
            y1stage(i - 1)
        if 2 <= i < 10:
            y2stage(i - 2)
        if i >= LAG:
            attention(i - LAG)
        if 2 <= i < 2 + len(w_events):
            wevent(*w_events[i - 2])
    me = y * 2 + k

    @pl.loop(0, B)
    def _(b):
        out = (ACC[b] / jnp.sum(L[b], axis=1, keepdims=True)).astype(jnp.bfloat16)
        rows = pl.ds(pl.multiple_of(b * T, T), T)
        for h in range(G):
            A[me, rows, h * HEAD_DIM:(h + 1) * HEAD_DIM] = out[h * T:(h + 1) * T]

    def ac(side, h, yy):
        d = A.at[yy * 2 + k].at[h * HT:(h + 1) * HT]
        return remote(d, d, sa.at[side, h], ra.at[side, h], y=yp if side == 0 else ym)

    def hop(side, yy):
        d = A.at[yy * 2 + k].at[side * HT:(side + 1) * HT]
        return remote(d, d, sh.at[side], rh.at[side], y=yp if side == 0 else ym)

    def asib(i, kk):
        d = A.at[ys[i] * 2 + kk]
        return remote(d, d, sas.at[i], ras.at[i], core=sib)

    asib(0, k).start()
    ac(0, 0, y).start()
    ac(1, 1, y).start()
    ac(0, 1, y).start()
    ac(1, 0, y).start()
    own_w.wait()

    R2 = 2 * NT

    def shard(d, p):
        return 2 * ((x + d) % XN) + p

    def compute(r, d):
        rows = A[pl.ds(ys[r] * 2, 2)].reshape(R2, KD)
        for p in (0, 1):
            res = jnp.dot(rows, W[shard(d, p)], preferred_element_type=jnp.float32)
            PB[r, d, p] = res.astype(jnp.bfloat16).reshape(2, NT, 128)

    def to_adjacent(r, p):
        return remote(PB.at[r, 2, p], RO.at[r, p], sx.at[r, p], rx.at[r, p], head=xp if p == 0 else xm)

    def to_dest(r, side, p):
        return remote(PB.at[r, 1 if side == 0 else 3, p], RA.at[r, side, p], sr.at[r, side, p], rr.at[r, side, p],
                      head=xp if side == 0 else xm)

    def project(r):
        compute(r, 2)
        to_adjacent(r, 0).start()
        to_adjacent(r, 1).start()
        compute(r, 1)
        to_dest(r, 0, 1).start()
        compute(r, 3)
        to_dest(r, 1, 0).start()
        compute(r, 0)

    def middle(r):
        for side, p in ((0, 0), (1, 1)):
            to_adjacent(r, p).wait_recv()
            d = 1 if side == 0 else 3
            PB[r, d, p] = (PB[r, d, p].astype(jnp.float32) + RO[r, p].astype(jnp.float32)).astype(jnp.bfloat16)
            to_dest(r, side, p).start()

    def column(p, yy, kk):
        return pl.ds(pl.multiple_of((p * 8 + yy * 2 + kk) * 128, 128), 128)

    def back(r, p, kk):
        return remote(FB.at[r, p, kk], o_ref.at[:, column(p, y, k)], so.at[r, p, 0], ro.at[r, p, 0],
                      y=ys[r], core=kk)

    def back_to(r, p, dk):
        kk = (k + dk) % 2
        return remote(FB.at[r, p, kk], o_ref.at[:, column(p, y, k)], so.at[r, p, dk], ro.at[r, p, dk],
                      y=ys[r], core=kk)

    def back_from(r, p, dk):
        kk = (k + dk) % 2
        src_y = (y, yp, ym, y2)[r]
        return remote(FB.at[r, p, 0], o_ref.at[:, column(p, src_y, kk)], so.at[r, p, dk], ro.at[r, p, dk],
                      y=y2, core=kk)

    def own_back(p):
        return pltpu.make_async_copy(FB.at[0, p, k], o_ref.at[:, column(p, y, k)], lo.at[2 + p])

    def last(r):
        for p in (0, 1):
            to_dest(r, 0, p).wait_recv()
            to_dest(r, 1, p).wait_recv()
            FB[r, p] = (PB[r, 0, p].astype(jnp.float32) + RA[r, 0, p].astype(jnp.float32)
                        + RA[r, 1, p].astype(jnp.float32)).astype(jnp.bfloat16)
            for dk in (0, 1):
                if (r, dk) == (0, 0):
                    own_back(p).start()
                else:
                    back_to(r, p, dk).start()

    asib(0, sib).wait_recv()
    project(0)
    middle(0)
    ac(0, 0, ym).wait_recv()
    hop(0, ym).start()
    ac(1, 1, yp).wait_recv()
    hop(1, yp).start()
    ac(0, 1, ym).wait_recv()
    asib(1, k).start()
    ac(1, 0, yp).wait_recv()
    asib(2, k).start()
    asib(1, sib).wait_recv()
    project(1)
    asib(2, sib).wait_recv()
    project(2)
    last(0)
    middle(1)
    hop(0, y2).wait_recv()
    hop(1, y2).wait_recv()
    asib(3, k).start()
    middle(2)
    asib(3, sib).wait_recv()
    project(3)
    last(1)
    last(2)
    middle(3)
    last(3)

    for r in range(4):
        for p in (0, 1):
            for dk in (0, 1):
                if (r, dk) == (0, 0):
                    own_back(p).wait()
                else:
                    back_from(r, p, dk).wait_recv()
    for s in range(8):
        z_out[s].wait_send()
        yc(s, 0, y).wait_send()
        yc(s, 1, y).wait_send()
        yc2(s, 0, ym).wait_send()
        yc2(s, 1, yp).wait_send()
        for i in range(4):
            sc(s, i, k).wait_send()
    for dist in (1, 2, 3, 4):
        for side in (0, 1):
            for h in (0, 1):
                if dist < 4 or side == h:
                    wc(dist, side, h, z).wait_send()
    for i in (0, 1):
        for h in (0, 1):
            ac(i, h, y).wait_send()
        hop(i, y).wait_send()
    for i in range(4):
        asib(i, k).wait_send()
    for r in range(4):
        for p in (0, 1):
            to_adjacent(r, p).wait_send()
            for side in (0, 1):
                to_dest(r, side, p).wait_send()
            for dk in (0, 1):
                if (r, dk) != (0, 0):
                    back_to(r, p, dk).wait_send()


def layer(q, meta, kv, w_out, T=32):
    NT, width = q.shape
    N = kv.shape[0]
    KD = w_out.shape[0]
    any_ = pl.BlockSpec(memory_space=pl.ANY)
    vm = pl.BlockSpec(memory_space=pltpu.VMEM)
    dma = pltpu.SemaphoreType.DMA
    bf = jnp.bfloat16
    B, R = NT // T, T * (width // HEAD_DIM)
    return pl.pallas_call(
        functools.partial(layer_kernel, T),
        out_shape=jax.ShapeDtypeStruct((NT, 16 * 128), bf),
        in_specs=[vm, vm, any_, any_], out_specs=any_,
        scratch_shapes=[
            pltpu.VMEM((64, N, 128), bf), pltpu.VMEM((8, NT, KD), bf), pltpu.VMEM((8, KD, 128), bf),
            pltpu.VMEM((4, 4, 2, 2, NT, 128), bf), pltpu.VMEM((4, 2, 2, NT, 128), bf),
            pltpu.VMEM((4, 2, 2, 2, NT, 128), bf), pltpu.VMEM((4, 2, 2, NT, 128), bf),
            pltpu.VMEM((B, R, 128), jnp.float32), pltpu.VMEM((B, R, 128), jnp.float32),
            pltpu.VMEM((B, R, HEAD_DIM), jnp.float32),
            dma((8,)), dma((8,)), dma((8, 2)), dma((8, 2)), dma((8, 2)), dma((8, 2)), dma((8, 4)), dma((8, 4)),
            dma((4, 2, 2)), dma((4, 2, 2)),
            dma((2, 2)), dma((2, 2)), dma((2,)), dma((2,)), dma((4,)), dma((4,)),
            dma((4, 2)), dma((4, 2)), dma((4, 2, 2)), dma((4, 2, 2)), dma((4, 2, 2)), dma((4, 2, 2)), dma((4,)),
        ],
        compiler_params=pltpu.CompilerParams(collective_id=0, has_side_effects=True, vmem_limit_bytes=48 << 20),
    )(q, meta, kv, w_out)


CTX = ("z", "y", "core")


def body(queries, keys, values, doc_ids, plan, w_out):
    n_rows, width = queries.shape
    parts = 64
    piece = n_rows // parts
    id_rows = jnp.pad(doc_ids.astype(jnp.bfloat16)[None, :], ((0, 15), (0, 0)))
    kv = jnp.concatenate([keys, values, id_rows], axis=0)
    local = jnp.arange(n_rows, dtype=jnp.int32).astype(jnp.bfloat16)
    extra = jnp.pad(
        jnp.stack([local, doc_ids.astype(jnp.bfloat16)], axis=1), ((0, 0), (0, 126))
    )
    rows = jnp.concatenate([queries, extra], axis=1).reshape(parts, piece, width + 128)
    rows = jnp.take(rows, plan[0], axis=0, mode="clip")
    moved = lax.all_to_all(rows, CTX, split_axis=0, concat_axis=0, tiled=True)
    moved = moved.reshape(n_rows, width + 128)
    meta = moved[:, width : width + 2].astype(jnp.float32)
    first = (jnp.arange(n_rows) // piece * n_rows).astype(jnp.float32)
    meta = meta + jnp.stack([first, jnp.zeros_like(first)], axis=1)
    return layer(moved[:, :width], meta, kv, w_out)


def solution(mesh):
    fine = Mesh(mesh.devices.reshape(ZN, YN, 2, XN), CTX + ("head",))
    return jax.shard_map(
        body,
        mesh=fine,
        in_specs=(
            P(CTX, "head"),
            P(CTX, "head"),
            P(CTX, "head"),
            P(CTX),
            P(CTX, None),
            P("head", CTX),
        ),
        out_specs=P(CTX, "head"),
        check_vma=False,
    )
```

```python
import functools
import math

import jax
import jax.numpy as jnp
from jax import lax
from jax.experimental import pallas as pl
from jax.experimental.pallas import tpu as pltpu
from jax.sharding import Mesh, PartitionSpec as P

HEAD_DIM = 128
NEG_FILL = -1e30

MESH = pl.DeviceIdType.MESH
STEPS = (0, -1, 1, -2, 2, -3, 3, 4)
ZN, YN, XN = 8, 4, 4


def remote(src, dst, send, recv, **where):
    return pltpu.make_async_remote_copy(
        src_ref=src, dst_ref=dst, send_sem=send, recv_sem=recv,
        device_id=where, device_id_type=MESH)


def layer_kernel(T, q_ref, k_ref, v_ref, id_ref, plan_ref, w_ref, o_ref,
                 KV, A, W, PB, RO, RA, FB, M, L, ACC, IDS, QF, QS, QR, Q2, MS, MR, META,
                 sq, rq, sm, rm,
                 sz, rz, sy, ry, sy2, ry2, ss, rs, sw, rw,
                 sa, ra, sh, rh, sas, ras, sx, rx, sr, rr, so, ro, lo):
    z, y, k, x = (lax.axis_index(n) for n in ("z", "y", "core", "head"))
    zp, zm = (z + 1) % ZN, (z + ZN - 1) % ZN
    yp, ym, y2 = (y + 1) % YN, (y + YN - 1) % YN, (y + 2) % YN
    xp, xm = (x + 1) % XN, (x + XN - 1) % XN
    sib = 1 - k
    NT = q_ref.shape[0]
    G = q_ref.shape[1] // HEAD_DIM
    N = KV.shape[1]
    KD = w_ref.shape[0]
    H, HT, HK = 128, NT // 2, KD // 2
    zs = [(z + d + ZN) % ZN for d in STEPS]
    ys = (y, ym, yp, y2)

    me = (z * YN + y) * 2 + k
    P64 = NT // 2

    barrier = pltpu.get_barrier_semaphore()

    def place(d):
        return {"z": d // (2 * YN), "y": (d // 2) % YN, "core": d % 2}

    for to in (xp, xm):
        pl.semaphore_signal(barrier, inc=1, device_id={"head": to}, device_id_type=MESH)

    @pl.loop(1, P64)
    def _(o):
        pl.semaphore_signal(barrier, inc=1, device_id=place((me + o) % P64), device_id_type=MESH)

    group = [(dy, dk) for dy in range(YN) for dk in range(2) if (dy, dk) != (0, 0)]
    IDS[...] = jnp.broadcast_to(id_ref[...].astype(jnp.float32), (16, NT)).astype(jnp.bfloat16)
    own_k = pltpu.make_async_copy(k_ref, KV.at[me].at[0:NT], lo.at[0])
    own_v = pltpu.make_async_copy(v_ref, KV.at[me].at[NT:2 * NT], lo.at[1])
    own_k.start()
    own_v.start()

    row = lax.broadcasted_iota(jnp.int32, (NT, NT), 0)
    lane = lax.broadcasted_iota(jnp.int32, (NT, NT), 1)
    wanted = plan_ref[...] * 2
    wanted = jnp.concatenate([wanted, wanted + 1], axis=1)
    pick = jnp.where(row == wanted, 1.0, 0.0).astype(jnp.bfloat16)
    across = (((0,), (0,)), ((), ()))
    for h in range(G):
        part = lax.dot_general(pick, q_ref[:, h * HEAD_DIM:(h + 1) * HEAD_DIM], across,
                               preferred_element_type=jnp.float32)
        for i in (0, 1):
            QF[pl.ds(2 * h + i, P64, stride=16), :] = part[i * P64:(i + 1) * P64]
    QS[...] = QF[...].astype(jnp.bfloat16).reshape(P64, 16, HEAD_DIM)
    doc = jnp.sum(jnp.where(row == lane, id_ref[...], 0), axis=1, keepdims=True)
    both = 0.0
    for i in (0, 1):
        told = jnp.where(lane == 2 * i, row, jnp.where(lane == 2 * i + 1, doc, 0)).astype(jnp.float32)
        both = both + lax.dot_general(pick[:, i * P64:(i + 1) * P64], told.astype(jnp.bfloat16), across,
                                      preferred_element_type=jnp.float32)
    for j in range(P64):
        MS[j] = both[j:j + 1]

    pl.semaphore_wait(barrier, P64 + 1)

    def slot(zz, yy, kk):
        return KV.at[(zz * YN + yy) * 2 + kk]

    def zc(i, zz, a, b, to, src=None):
        d = slot(zz, y, k).at[a:b]
        return remote(d if src is None else src, d, sz.at[i], rz.at[i], z=to)

    z_out = [zc(0, z, 0, N, zp), zc(1, z, 0, N, zm),
             zc(2, zs[1], 0, N, zp), zc(3, zs[2], 0, N, zm),
             zc(4, zs[3], 0, N, zp), zc(5, zs[4], 0, N, zm),
             zc(6, zs[5], 0, H, zp), zc(7, zs[6], H, N, zm)]
    z_in = [zc(0, zs[1], 0, N, zp), zc(1, zs[2], 0, N, zm),
            zc(2, zs[3], 0, N, zp), zc(3, zs[4], 0, N, zm),
            zc(4, zs[5], 0, N, zp), zc(5, zs[6], 0, N, zm),
            zc(6, zs[7], 0, H, zp), zc(7, zs[7], H, N, zm)]

    def yc(s, side, yy, src=None):
        d = slot(zs[s], yy, k)
        return remote(d if src is None else src, d, sy.at[s, side], ry.at[s, side], y=yp if side == 0 else ym)

    def yc2(s, side, yy):
        d = slot(zs[s], yy, k)
        d = d.at[0:H] if side == 0 else d.at[H:N]
        return remote(d, d, sy2.at[s, side], ry2.at[s, side], y=yp if side == 0 else ym)

    def sc(s, i, kk, src=None):
        d = slot(zs[s], ys[i], kk)
        return remote(d if src is None else src, d, ss.at[s, i], rs.at[s, i], core=sib)

    own_ids = pltpu.make_async_copy(IDS, KV.at[me].at[2 * NT:N], lo.at[4])

    def piece(o):
        d = (me + o) % P64
        return (remote(QS.at[d], QR.at[me], sq.at[o], rq.at[o], **place(d)),
                remote(MS.at[d], MR.at[me], sm.at[o], rm.at[o], **place(d)))

    def piece_in(o):
        d = (me + P64 - o) % P64
        return (remote(QS.at[d], QR.at[d], sq.at[o], rq.at[o], **place(d)),
                remote(MS.at[d], MR.at[d], sm.at[o], rm.at[o], **place(d)))

    own_q = pltpu.make_async_copy(QS.at[me], QR.at[me], lo.at[5])
    own_m = pltpu.make_async_copy(MS.at[me], MR.at[me], lo.at[6])

    def send_queries():
        own_q.start()
        own_m.start()

        @pl.loop(1, P64)
        def _(o):
            for cp in piece(o):
                cp.start()

    def take_queries():
        own_q.wait()
        own_m.wait()

        @pl.loop(1, P64)
        def _(o):
            for cp in piece_in(o):
                cp.wait_recv()

        QF[...] = QR[...].astype(jnp.float32).reshape(P64 * 16, HEAD_DIM)
        for b in range(B):
            PB_ = T // 2
            q = [QF[pl.ds(b * PB_ * 16 + 2 * h + i, PB_, stride=16), :] for h in range(G) for i in (0, 1)]
            Q2[b] = jnp.concatenate(q, axis=0).astype(jnp.bfloat16)
            told = jnp.concatenate([MR[j] for j in range(b * PB_, (b + 1) * PB_)], axis=0)
            first = ((b * PB_ + lax.broadcasted_iota(jnp.int32, (PB_, 1), 0)) * NT).astype(jnp.float32)
            for i in (0, 1):
                META[b, i * PB_:(i + 1) * PB_, :] = jnp.concatenate(
                    [jnp.broadcast_to(told[:, 2 * i:2 * i + 1] + first, (PB_, 128)),
                     jnp.broadcast_to(told[:, 2 * i + 1:2 * i + 2], (PB_, 128))], axis=1)

    B = NT // T

    def wc(dist, side, h, src_z, src=None):
        d = W.at[src_z].at[h * HK:(h + 1) * HK]
        return remote(d if src is None else src, d, sw.at[dist - 1, side, h], rw.at[dist - 1, side, h],
                      z=zp if side == 0 else zm)

    def zat(side, dist):
        return (z + (ZN - dist if side == 0 else dist)) % ZN

    own_w = pltpu.make_async_copy(w_ref, W.at[z], lo.at[7])

    def wstart():
        for h in (0, 1):
            for side in (0, 1):
                wc(1, side, h, z, w_ref.at[h * HK:(h + 1) * HK]).start()
        own_w.start()

    def wevent(dist, h):
        for side in (0, 1):
            if dist == 4 and side != h:
                continue
            src = zat(side, dist)
            wc(dist, side, h, src).wait_recv()
            if dist < 3 or (dist == 3 and side == h):
                wc(dist + 1, side, h, src).start()

    w_events = [(d, h) for d in (1, 2, 3, 4) for h in (0, 1)]

    def zstage(s):
        src = None
        if s == 0:
            own_k.wait()
            own_v.wait()
            own_ids.start()
            own_ids.wait()
            z_out[0].start()
            z_out[1].start()
        elif s == 7:
            z_in[6].wait_recv()
            z_in[7].wait_recv()
        else:
            z_in[s - 1].wait_recv()
            z_out[s + 1].start()
        yc(s, 0, y, src).start()
        yc(s, 1, y, src).start()
        sc(s, 0, k, src).start()
        if s == 0:
            send_queries()
            wstart()

    def y1stage(s):
        yc(s, 0, ym).wait_recv()
        yc2(s, 0, ym).start()
        sc(s, 1, k).start()
        yc(s, 1, yp).wait_recv()
        yc2(s, 1, yp).start()
        sc(s, 2, k).start()

    def y2stage(s):
        yc2(s, 0, y2).wait_recv()
        yc2(s, 1, y2).wait_recv()
        sc(s, 3, k).start()

    R = G * T
    TK = 2 * YN * 128
    c = math.log2(math.e) / math.sqrt(HEAD_DIM)
    M[...] = jnp.full_like(M, NEG_FILL)
    L[...] = jnp.zeros_like(L)
    ACC[...] = jnp.zeros_like(ACC)

    def attention(s):
        if s == 0:
            take_queries()
        for i in range(4):
            sc(s, i, sib).wait_recv()
        zz = zs[s]
        base = zz * 2 * YN

        def unit(b, carry):
            q = Q2[b]
            pos, doc = META[b][:, 0:1], META[b][:, 128:129]
            kk = KV[pl.ds(base, 2 * YN), 0:128, :].reshape(TK, HEAD_DIM)
            vv = KV[pl.ds(base, 2 * YN), 128:256, :].reshape(TK, HEAD_DIM)
            ids = jnp.concatenate([KV[base + i, 256:272, :].astype(jnp.float32)[0:1] for i in range(2 * YN)], axis=1)
            u = (zz * TK + lax.broadcasted_iota(jnp.int32, (T, TK), 1)).astype(jnp.float32)
            ok = (ids == doc) & (u <= pos)
            sco = lax.dot_general(q, kk, (((1,), (1,)), ((), ())), preferred_element_type=jnp.float32)
            sco = jnp.where(ok[None], sco.reshape(G, T, TK), NEG_FILL).reshape(R, TK)
            m = M[b][:, 0:1]
            m_new = jnp.maximum(m, jnp.max(sco, axis=1, keepdims=True))
            p = jnp.exp2((sco - m_new) * c)
            a = jnp.exp2((m - m_new) * c)
            part = p[:, 0:128]
            for i in range(1, TK // 128):
                part = part + p[:, i * 128:(i + 1) * 128]
            L[b] = L[b] * a + part
            ACC[b] = ACC[b] * a + jnp.dot(p.astype(jnp.bfloat16), vv, preferred_element_type=jnp.float32)
            M[b] = jnp.broadcast_to(m_new, (R, 128))
            return carry

        per = T * 64 // TK
        lax.fori_loop(zz // per, B, unit, 0)

    LAG = 3
    for i in range(8 + LAG):
        if i < 8:
            zstage(i)
        if 1 <= i < 9:
            y1stage(i - 1)
        if 2 <= i < 10:
            y2stage(i - 2)
        if i >= LAG:
            attention(i - LAG)
        if 2 <= i < 2 + len(w_events):
            wevent(*w_events[i - 2])
    mine = y * 2 + k
    tr, tc = lax.broadcasted_iota(jnp.int32, (T, T), 0), lax.broadcasted_iota(jnp.int32, (T, T), 1)
    order = jnp.where((tr % 2) * (T // 2) + tr // 2 == tc, 1.0, 0.0).astype(jnp.bfloat16)

    @pl.loop(0, B)
    def _(b):
        out = (ACC[b] / jnp.sum(L[b], axis=1, keepdims=True)).astype(jnp.bfloat16)
        rows = pl.ds(pl.multiple_of(b * T, T), T)
        out = jnp.concatenate([out[h * T:(h + 1) * T] for h in range(G)], axis=1)
        A[mine, rows, :] = jnp.dot(order, out, preferred_element_type=jnp.float32).astype(jnp.bfloat16)

    def ac(side, h, yy):
        d = A.at[yy * 2 + k].at[h * HT:(h + 1) * HT]
        return remote(d, d, sa.at[side, h], ra.at[side, h], y=yp if side == 0 else ym)

    def hop(side, yy):
        d = A.at[yy * 2 + k].at[side * HT:(side + 1) * HT]
        return remote(d, d, sh.at[side], rh.at[side], y=yp if side == 0 else ym)

    def asib(i, kk):
        d = A.at[ys[i] * 2 + kk]
        return remote(d, d, sas.at[i], ras.at[i], core=sib)

    asib(0, k).start()
    ac(0, 0, y).start()
    ac(1, 1, y).start()
    ac(0, 1, y).start()
    ac(1, 0, y).start()
    own_w.wait()

    R2 = 2 * NT

    def shard(d, p):
        return 2 * ((x + d) % XN) + p

    def compute(r, d):
        rows = A[pl.ds(ys[r] * 2, 2)].reshape(R2, KD)
        for p in (0, 1):
            res = jnp.dot(rows, W[shard(d, p)], preferred_element_type=jnp.float32)
            PB[r, d, p] = res.astype(jnp.bfloat16).reshape(2, NT, 128)

    def to_adjacent(r, p):
        return remote(PB.at[r, 2, p], RO.at[r, p], sx.at[r, p], rx.at[r, p], head=xp if p == 0 else xm)

    def to_dest(r, side, p):
        return remote(PB.at[r, 1 if side == 0 else 3, p], RA.at[r, side, p], sr.at[r, side, p], rr.at[r, side, p],
                      head=xp if side == 0 else xm)

    def project(r):
        compute(r, 2)
        to_adjacent(r, 0).start()
        to_adjacent(r, 1).start()
        compute(r, 1)
        to_dest(r, 0, 1).start()
        compute(r, 3)
        to_dest(r, 1, 0).start()
        compute(r, 0)

    def middle(r):
        for side, p in ((0, 0), (1, 1)):
            to_adjacent(r, p).wait_recv()
            d = 1 if side == 0 else 3
            PB[r, d, p] = (PB[r, d, p].astype(jnp.float32) + RO[r, p].astype(jnp.float32)).astype(jnp.bfloat16)
            to_dest(r, side, p).start()

    def column(p, yy, kk):
        return pl.ds(pl.multiple_of((p * 8 + yy * 2 + kk) * 128, 128), 128)

    def back(r, p, kk):
        return remote(FB.at[r, p, kk], o_ref.at[:, column(p, y, k)], so.at[r, p, 0], ro.at[r, p, 0],
                      y=ys[r], core=kk)

    def back_to(r, p, dk):
        kk = (k + dk) % 2
        return remote(FB.at[r, p, kk], o_ref.at[:, column(p, y, k)], so.at[r, p, dk], ro.at[r, p, dk],
                      y=ys[r], core=kk)

    def back_from(r, p, dk):
        kk = (k + dk) % 2
        src_y = (y, yp, ym, y2)[r]
        return remote(FB.at[r, p, 0], o_ref.at[:, column(p, src_y, kk)], so.at[r, p, dk], ro.at[r, p, dk],
                      y=y2, core=kk)

    def own_back(p):
        return pltpu.make_async_copy(FB.at[0, p, k], o_ref.at[:, column(p, y, k)], lo.at[2 + p])

    def last(r):
        for p in (0, 1):
            to_dest(r, 0, p).wait_recv()
            to_dest(r, 1, p).wait_recv()
            FB[r, p] = (PB[r, 0, p].astype(jnp.float32) + RA[r, 0, p].astype(jnp.float32)
                        + RA[r, 1, p].astype(jnp.float32)).astype(jnp.bfloat16)
            for dk in (0, 1):
                if (r, dk) == (0, 0):
                    own_back(p).start()
                else:
                    back_to(r, p, dk).start()

    asib(0, sib).wait_recv()
    project(0)
    middle(0)
    ac(0, 0, ym).wait_recv()
    hop(0, ym).start()
    ac(1, 1, yp).wait_recv()
    hop(1, yp).start()
    ac(0, 1, ym).wait_recv()
    asib(1, k).start()
    ac(1, 0, yp).wait_recv()
    asib(2, k).start()
    asib(1, sib).wait_recv()
    project(1)
    asib(2, sib).wait_recv()
    project(2)
    last(0)
    middle(1)
    hop(0, y2).wait_recv()
    hop(1, y2).wait_recv()
    asib(3, k).start()
    middle(2)
    asib(3, sib).wait_recv()
    project(3)
    last(1)
    last(2)
    middle(3)
    last(3)

    for r in range(4):
        for p in (0, 1):
            for dk in (0, 1):
                if (r, dk) == (0, 0):
                    own_back(p).wait()
                else:
                    back_from(r, p, dk).wait_recv()
    @pl.loop(1, P64)
    def _(o):
        for cp in piece(o):
            cp.wait_send()

    for s in range(8):
        z_out[s].wait_send()
        yc(s, 0, y).wait_send()
        yc(s, 1, y).wait_send()
        yc2(s, 0, ym).wait_send()
        yc2(s, 1, yp).wait_send()
        for i in range(4):
            sc(s, i, k).wait_send()
    for dist in (1, 2, 3, 4):
        for side in (0, 1):
            for h in (0, 1):
                if dist < 4 or side == h:
                    wc(dist, side, h, z).wait_send()
    for i in (0, 1):
        for h in (0, 1):
            ac(i, h, y).wait_send()
        hop(i, y).wait_send()
    for i in range(4):
        asib(i, k).wait_send()
    for r in range(4):
        for p in (0, 1):
            to_adjacent(r, p).wait_send()
            for side in (0, 1):
                to_dest(r, side, p).wait_send()
            for dk in (0, 1):
                if (r, dk) != (0, 0):
                    back_to(r, p, dk).wait_send()


def layer(q, keys, values, ids, plan, w_out, T=32):
    NT, width = q.shape
    N = 2 * NT + 16
    KD = w_out.shape[0]
    any_ = pl.BlockSpec(memory_space=pl.ANY)
    vm = pl.BlockSpec(memory_space=pltpu.VMEM)
    dma = pltpu.SemaphoreType.DMA
    bf, f32 = jnp.bfloat16, jnp.float32
    B, R, P64 = NT // T, T * (width // HEAD_DIM), NT // 2
    return pl.pallas_call(
        functools.partial(layer_kernel, T),
        out_shape=jax.ShapeDtypeStruct((NT, 16 * 128), bf),
        in_specs=[vm, any_, any_, vm, vm, any_], out_specs=any_,
        scratch_shapes=[
            pltpu.VMEM((64, N, 128), bf), pltpu.VMEM((8, NT, KD), bf), pltpu.VMEM((8, KD, 128), bf),
            pltpu.VMEM((4, 4, 2, 2, NT, 128), bf), pltpu.VMEM((4, 2, 2, NT, 128), bf),
            pltpu.VMEM((4, 2, 2, 2, NT, 128), bf), pltpu.VMEM((4, 2, 2, NT, 128), bf),
            pltpu.VMEM((B, R, 128), f32), pltpu.VMEM((B, R, 128), f32), pltpu.VMEM((B, R, HEAD_DIM), f32),
            pltpu.VMEM((16, NT), bf), pltpu.VMEM((P64 * 16, HEAD_DIM), f32),
            pltpu.VMEM((P64, 16, HEAD_DIM), bf), pltpu.VMEM((P64, 16, HEAD_DIM), bf), pltpu.VMEM((B, R, HEAD_DIM), bf),
            pltpu.VMEM((P64, 1, 128), f32), pltpu.VMEM((P64, 1, 128), f32), pltpu.VMEM((B, T, 256), f32),
            dma((64,)), dma((64,)), dma((64,)), dma((64,)),
            dma((8,)), dma((8,)), dma((8, 2)), dma((8, 2)), dma((8, 2)), dma((8, 2)), dma((8, 4)), dma((8, 4)),
            dma((4, 2, 2)), dma((4, 2, 2)),
            dma((2, 2)), dma((2, 2)), dma((2,)), dma((2,)), dma((4,)), dma((4,)),
            dma((4, 2)), dma((4, 2)), dma((4, 2, 2)), dma((4, 2, 2)), dma((4, 2, 2)), dma((4, 2, 2)), dma((8,)),
        ],
        compiler_params=pltpu.CompilerParams(collective_id=0, has_side_effects=True, vmem_limit_bytes=48 << 20),
    )(q, keys, values, ids, plan, w_out)


CTX = ("z", "y", "core")


def body(queries, keys, values, doc_ids, plan, w_out):
    return layer(queries, keys, values, doc_ids.reshape(1, -1), plan, w_out)


def solution(mesh):
    fine = Mesh(mesh.devices.reshape(ZN, YN, 2, XN), CTX + ("head",))
    return jax.shard_map(
        body,
        mesh=fine,
        in_specs=(
            P(CTX, "head"),
            P(CTX, "head"),
            P(CTX, "head"),
            P(CTX),
            P(CTX, None),
            P("head", CTX),
        ),
        out_specs=P(CTX, "head"),
        check_vma=False,
    )
```

```python
import functools
import math

import jax
import jax.numpy as jnp
from jax import lax
from jax.experimental import pallas as pl
from jax.experimental.pallas import tpu as pltpu
from jax.sharding import Mesh, PartitionSpec as P

HEAD_DIM = 128
NEG_FILL = -1e30

MESH = pl.DeviceIdType.MESH
STEPS = (0, -1, 1, -2, 2, -3, 3, 4)
ZN, YN, XN = 8, 4, 4


def remote(src, dst, send, recv, **where):
    return pltpu.make_async_remote_copy(
        src_ref=src, dst_ref=dst, send_sem=send, recv_sem=recv,
        device_id=where, device_id_type=MESH)


def layer_kernel(T, WC, plan_a, q_ref, k_ref, v_ref, id_ref, plan_ref, w_ref, o_ref,
                 KV, A, W, PB, RO, RA, FB, M, L, ACC, PR, QF, QS, QR, Q2, MS, MR, META,
                 sq, rq, sm, rm, skv, rz, ry, ry2, rs, sw, rw,
                 sa, ra, rh, ras, sx, rx, rr, so, ro, lo):
    z, y, k, x = (lax.axis_index(n) for n in ("z", "y", "core", "head"))
    zp, zm = (z + 1) % ZN, (z + ZN - 1) % ZN
    yp, ym, y2 = (y + 1) % YN, (y + YN - 1) % YN, (y + 2) % YN
    xp, xm = (x + 1) % XN, (x + XN - 1) % XN
    sib = 1 - k
    NT = q_ref.shape[0]
    G = q_ref.shape[1] // HEAD_DIM
    N = KV.shape[1]
    KD = w_ref.shape[0]
    H, HT, HK = 128, NT // 2, KD // WC
    zs = [(z + d + ZN) % ZN for d in STEPS]
    ys = (y, ym, yp, y2)

    me = (z * YN + y) * 2 + k

    def sent(ref, sem):
        remote(ref, ref, sem, sem, core=1 - k).wait_send()

    def arrived(ref, sem):
        remote(ref, ref, sem, sem, core=1 - k).wait_recv()

    P64 = NT // 2

    barrier = pltpu.get_barrier_semaphore()

    def place(d):
        return {"z": d // (2 * YN), "y": (d // 2) % YN, "core": d % 2}

    for to in (xp, xm):
        pl.semaphore_signal(barrier, inc=1, device_id={"head": to}, device_id_type=MESH)

    @pl.loop(1, P64)
    def _(o):
        pl.semaphore_signal(barrier, inc=1, device_id=place((me + o) % P64), device_id_type=MESH)

    group = [(dy, dk) for dy in range(YN) for dk in range(2) if (dy, dk) != (0, 0)]
    KV[me, 2 * NT:N, :] = jnp.broadcast_to(id_ref[...].astype(jnp.float32), (16, NT)).astype(jnp.bfloat16)
    own_k = pltpu.make_async_copy(k_ref, KV.at[me].at[0:NT], lo.at[0])
    own_v = pltpu.make_async_copy(v_ref, KV.at[me].at[NT:2 * NT], lo.at[1])
    own_k.start()
    own_v.start()

    row = lax.broadcasted_iota(jnp.int32, (NT, NT), 0)
    lane = lax.broadcasted_iota(jnp.int32, (NT, NT), 1)
    wanted = plan_ref[...] * 2
    wanted = jnp.concatenate([wanted, wanted + 1], axis=1)
    pick = jnp.where(row == wanted, 1.0, 0.0).astype(jnp.bfloat16)
    across = (((0,), (0,)), ((), ()))
    for h in range(G):
        part = lax.dot_general(pick, q_ref[:, h * HEAD_DIM:(h + 1) * HEAD_DIM], across,
                               preferred_element_type=jnp.float32)
        for i in (0, 1):
            QF[pl.ds(2 * h + i, P64, stride=16), :] = part[i * P64:(i + 1) * P64]
    QS[...] = QF[...].astype(jnp.bfloat16).reshape(P64, 16, HEAD_DIM)
    doc = jnp.sum(jnp.where(row == lane, id_ref[...], 0), axis=1, keepdims=True)
    both = 0.0
    for i in (0, 1):
        told = jnp.where(lane == 2 * i, row, jnp.where(lane == 2 * i + 1, doc, 0)).astype(jnp.float32)
        both = both + lax.dot_general(pick[:, i * P64:(i + 1) * P64], told.astype(jnp.bfloat16), across,
                                      preferred_element_type=jnp.float32)
    for j in range(P64):
        MS[j] = both[j:j + 1]

    pl.semaphore_wait(barrier, P64 + 1)

    def slot(zz, yy, kk):
        return KV.at[(zz * YN + yy) * 2 + kk]

    def zc(i, zz, a, b, to, src=None):
        d = slot(zz, y, k).at[a:b]
        return remote(d if src is None else src, d, skv, rz.at[i], z=to)

    z_out = [zc(0, z, 0, N, zp), zc(1, z, 0, N, zm),
             zc(2, zs[1], 0, N, zp), zc(3, zs[2], 0, N, zm),
             zc(4, zs[3], 0, N, zp), zc(5, zs[4], 0, N, zm),
             zc(6, zs[5], 0, H, zp), zc(7, zs[6], H, N, zm)]
    z_in = [zc(0, zs[1], 0, N, zp), zc(1, zs[2], 0, N, zm),
            zc(2, zs[3], 0, N, zp), zc(3, zs[4], 0, N, zm),
            zc(4, zs[5], 0, N, zp), zc(5, zs[6], 0, N, zm),
            zc(6, zs[7], 0, H, zp), zc(7, zs[7], H, N, zm)]

    def yc(s, side, yy, src=None):
        d = slot(zs[s], yy, k)
        return remote(d if src is None else src, d, skv, ry.at[s], y=yp if side == 0 else ym)

    def yc2(s, side, yy):
        d = slot(zs[s], yy, k)
        d = d.at[0:H] if side == 0 else d.at[H:N]
        return remote(d, d, skv, ry2.at[s], y=yp if side == 0 else ym)

    def sc(s, i, kk, src=None):
        d = slot(zs[s], ys[i], kk)
        return remote(d if src is None else src, d, skv, rs.at[s], core=sib)


    def piece(o):
        d = (me + o) % P64
        return (remote(QS.at[d], QR.at[me], sq, rq, **place(d)),
                remote(MS.at[d], MR.at[me], sm, rm, **place(d)))

    own_q = pltpu.make_async_copy(QS.at[me], QR.at[me], lo.at[5])
    own_m = pltpu.make_async_copy(MS.at[me], MR.at[me], lo.at[6])

    def send_queries():
        own_q.start()
        own_m.start()

        @pl.loop(1, P64)
        def _(o):
            for cp in piece(o):
                cp.start()

    def take_queries():
        own_q.wait()
        own_m.wait()

        arrived(QR.at[0:P64 - 1], rq)
        arrived(MR.at[0:P64 - 1], rm)
        QF[...] = QR[...].astype(jnp.float32).reshape(P64 * 16, HEAD_DIM)
        for b in range(B):
            PB_ = T // 2
            q = [QF[pl.ds(b * PB_ * 16 + 2 * h + i, PB_, stride=16), :] for h in range(G) for i in (0, 1)]
            Q2[b] = jnp.concatenate(q, axis=0).astype(jnp.bfloat16)
            told = jnp.concatenate([MR[j] for j in range(b * PB_, (b + 1) * PB_)], axis=0)
            first = ((b * PB_ + lax.broadcasted_iota(jnp.int32, (PB_, 1), 0)) * NT).astype(jnp.float32)
            for i in (0, 1):
                META[b, i * PB_:(i + 1) * PB_, :] = jnp.concatenate(
                    [jnp.broadcast_to(told[:, 2 * i:2 * i + 1] + first, (PB_, 128)),
                     jnp.broadcast_to(told[:, 2 * i + 1:2 * i + 2], (PB_, 128))], axis=1)

    B = NT // T

    def wslot(zz, h):
        return W.at[zz // 2].at[h * HK:(h + 1) * HK, pl.ds(pl.multiple_of((zz % 2) * 128, 128), 128)]

    def wc(dist, side, h, src_z, src=None):
        d = wslot(src_z, h)
        return remote(d if src is None else src, d, sw, rw.at[dist - 1, h], z=zp if side == 0 else zm)

    def zat(side, dist):
        return (z + (ZN - dist if side == 0 else dist)) % ZN

    own_w = pltpu.make_async_copy(
        w_ref, W.at[z // 2].at[:, pl.ds(pl.multiple_of((z % 2) * 128, 128), 128)], lo.at[7])

    def wstart(h):
        for side in (0, 1):
            wc(1, side, h, z, w_ref.at[h * HK:(h + 1) * HK]).start()
        if h == WC - 1:
            own_w.start()

    def wevent(dist, h):
        near = 0 if h < WC // 2 else 1
        if dist == 4:
            arrived(w_ref.at[0:HK], rw.at[3, h])
            return
        arrived(w_ref.at[0:2 * HK], rw.at[dist - 1, h])
        for side in (0, 1):
            if dist < 3 or side == near:
                wc(dist + 1, side, h, zat(side, dist)).start()

    def zstage(s):
        src = None
        if s == 0:
            own_k.wait()
            own_v.wait()
            z_out[0].start()
            z_out[1].start()
        elif s == 7:
            z_in[6].wait_recv()
            z_in[7].wait_recv()
        else:
            z_in[s - 1].wait_recv()
            z_out[s + 1].start()
        yc(s, 0, y, src).start()
        yc(s, 1, y, src).start()
        sc(s, 0, k, src).start()
        if s == 0:
            send_queries()

    def y1stage(s):
        arrived(KV.at[0:2], ry.at[s])
        yc2(s, 0, ym).start()
        yc2(s, 1, yp).start()
        sc(s, 1, k).start()
        sc(s, 2, k).start()

    def y2stage(s):
        arrived(KV.at[0], ry2.at[s])
        sc(s, 3, k).start()

    R = G * T
    TK = 2 * YN * 128
    c = math.log2(math.e) / math.sqrt(HEAD_DIM)
    M[...] = jnp.full_like(M, NEG_FILL)
    L[...] = jnp.zeros_like(L)
    ACC[...] = jnp.zeros_like(ACC)

    per = T * 64 // TK

    def attention(s):
        arrived(KV.at[0:4], rs.at[s])
        away = (s + 1) // 2
        zz = (z + jnp.where(s % 2 == 0, away, ZN - away)) % ZN
        base = zz * 2 * YN

        def against(b0):
            nb = B - b0
            kk = KV[pl.ds(base, 2 * YN), 0:128, :].reshape(TK, HEAD_DIM)
            ids = jnp.concatenate([KV[base + i, 256:272, :].astype(jnp.float32)[0:1] for i in range(2 * YN)], axis=1)
            u = (zz * TK + lax.broadcasted_iota(jnp.int32, (T, TK), 1)).astype(jnp.float32)
            sco = lax.dot_general(Q2[b0:B].reshape(nb * R, HEAD_DIM), kk, (((1,), (1,)), ((), ())),
                                  preferred_element_type=jnp.float32)
            for b in range(b0, B):
                pos, doc = META[b][:, 0:1], META[b][:, 128:129]
                ok = (ids == doc) & (u <= pos)
                sb = sco[(b - b0) * R:(b - b0 + 1) * R].reshape(G, T, TK)
                sb = jnp.where(ok[None], sb, NEG_FILL).reshape(R, TK)
                m = M[b][:, 0:1]
                m_new = jnp.maximum(m, jnp.max(sb, axis=1, keepdims=True))
                p = jnp.exp2((sb - m_new) * c)
                a = jnp.exp2((m - m_new) * c)
                part = p[:, 0:128]
                for i in range(1, TK // 128):
                    part = part + p[:, i * 128:(i + 1) * 128]
                L[b] = L[b] * a + part
                ACC[b] = ACC[b] * a
                M[b] = jnp.broadcast_to(m_new, (R, 128))
                PR[b] = p.astype(jnp.bfloat16)
            vv = KV[pl.ds(base, 2 * YN), 128:256, :].reshape(TK, HEAD_DIM)
            res = jnp.dot(PR[b0:B].reshape(nb * R, TK), vv, preferred_element_type=jnp.float32)
            ACC[b0:B] = ACC[b0:B] + res.reshape(nb, R, HEAD_DIM)

        for b0 in range(B):
            pl.when(zz // per == b0)(functools.partial(against, b0))

    steps = {"z": zstage, "y": y1stage, "Y": y2stage, "Q": take_queries, "W": wstart, "w": wevent}

    def run(events):
        for e in events.split():
            steps[e[0]](*(int(v) for v in e[1:]))

    @pl.loop(0, ZN)
    def _(s):
        for j in range(ZN):
            pl.when(s == j)(functools.partial(run, plan_a[j]))
        attention(s)

    mine = y * 2 + k
    tr, tc = lax.broadcasted_iota(jnp.int32, (T, T), 0), lax.broadcasted_iota(jnp.int32, (T, T), 1)
    order = jnp.where((tr % 2) * (T // 2) + tr // 2 == tc, 1.0, 0.0).astype(jnp.bfloat16)

    @pl.loop(0, B)
    def _(b):
        out = (ACC[b] / jnp.sum(L[b], axis=1, keepdims=True)).astype(jnp.bfloat16)
        rows = pl.ds(pl.multiple_of(b * T, T), T)
        out = jnp.concatenate([out[h * T:(h + 1) * T] for h in range(G)], axis=1)
        A[mine, rows, :] = jnp.dot(order, out, preferred_element_type=jnp.float32).astype(jnp.bfloat16)

    def ac(side, h, yy):
        d = A.at[yy * 2 + k].at[h * HT:(h + 1) * HT]
        return remote(d, d, sa, ra.at[side, h], y=yp if side == 0 else ym)

    def hop(side, yy):
        d = A.at[yy * 2 + k].at[side * HT:(side + 1) * HT]
        return remote(d, d, sa, rh, y=yp if side == 0 else ym)

    def asib(i, kk):
        whole = {0: y, 2: y2}
        if i in whole:
            parts = [A.at[whole[i] * 2 + kk]]
        else:
            h = (i - 1) // 2
            parts = [A.at[ym * 2 + kk].at[h * HT:(h + 1) * HT], A.at[yp * 2 + kk].at[(1 - h) * HT:(2 - h) * HT]]
        for d in parts:
            remote(d, d, sa, ras.at[i], core=sib).start()

    asib(0, k)
    ac(0, 0, y).start()
    ac(1, 1, y).start()
    run(plan_a[ZN])
    own_w.wait()

    R2 = 2 * NT

    def rows_of(r):
        if r in (0, 2):
            return A[pl.ds((y if r == 0 else y2) * 2, 2)].reshape(R2, KD)
        h = (r - 1) // 2
        return jnp.concatenate([A[pl.ds(ym * 2, 2), h * HT:(h + 1) * HT, :].reshape(NT, KD),
                                A[pl.ds(yp * 2, 2), (1 - h) * HT:(2 - h) * HT, :].reshape(NT, KD)], axis=0)

    def compute(r, d):
        res = jnp.dot(rows_of(r), W[(x + d) % XN], preferred_element_type=jnp.float32).astype(jnp.bfloat16)
        for p in (0, 1):
            PB[r, d, p] = res[:, p * 128:(p + 1) * 128]

    def to_adjacent(r, p):
        return remote(PB.at[r, 2, p], RO.at[r, p], sx, rx.at[r, p], head=xp if p == 0 else xm)

    def to_dest(r, side, p):
        return remote(PB.at[r, 1 if side == 0 else 3, p], RA.at[r, side, p], sx, rr.at[r, p],
                      head=xp if side == 0 else xm)

    def project(r):
        compute(r, 2)
        to_adjacent(r, 0).start()
        to_adjacent(r, 1).start()
        compute(r, 1)
        to_dest(r, 0, 1).start()
        compute(r, 3)
        to_dest(r, 1, 0).start()
        compute(r, 0)

    def middle(r):
        for side, p in ((0, 0), (1, 1)):
            to_adjacent(r, p).wait_recv()
            d = 1 if side == 0 else 3
            PB[r, d, p] = (PB[r, d, p].astype(jnp.float32) + RO[r, p].astype(jnp.float32)).astype(jnp.bfloat16)
            to_dest(r, side, p).start()

    def column(p, yy, kk):
        return pl.ds(pl.multiple_of((p * 8 + yy * 2 + kk) * 128, 128), 128)

    def back_to(r, p):
        col = column(p, y, k)
        if r == 0:
            return [remote(FB.at[0, p, pl.ds(pl.multiple_of(sib * NT, NT), NT)], o_ref.at[:, col], so, ro, core=sib)]
        out = []
        for kk in (0, 1):
            if r == 2:
                out.append(remote(FB.at[r, p, kk * NT:(kk + 1) * NT], o_ref.at[:, col], so, ro, y=y2, core=kk))
                continue
            h = (r - 1) // 2
            for n, (yy, hh) in enumerate(((ym, h), (yp, 1 - h))):
                at = n * NT + kk * HT
                out.append(remote(FB.at[r, p, at:at + HT], o_ref.at[hh * HT:(hh + 1) * HT, col], so, ro, y=yy, core=kk))
        return out

    def own_back(p):
        return pltpu.make_async_copy(FB.at[0, p, pl.ds(pl.multiple_of(k * NT, NT), NT)],
                                     o_ref.at[:, column(p, y, k)], lo.at[2 + p])

    def last(r):
        for p in (0, 1):
            arrived(RA.at[r, 0], rr.at[r, p])
            FB[r, p] = (PB[r, 0, p].astype(jnp.float32) + RA[r, 0, p].astype(jnp.float32)
                        + RA[r, 1, p].astype(jnp.float32)).astype(jnp.bfloat16)
            if r == 0:
                own_back(p).start()
            for cp in back_to(r, p):
                cp.start()

    def gathered(i):
        arrived(A.at[0], ras.at[i])

    gathered(0)
    project(0)
    ac(0, 0, ym).wait_recv()
    hop(0, ym).start()
    ac(1, 1, yp).wait_recv()
    hop(1, yp).start()
    asib(1, k)
    ac(0, 1, y).start()
    ac(1, 0, y).start()
    middle(0)
    gathered(1)
    project(1)
    last(0)
    arrived(A.at[0], rh)
    asib(2, k)
    middle(1)
    gathered(2)
    project(2)
    ac(0, 1, ym).wait_recv()
    ac(1, 0, yp).wait_recv()
    asib(3, k)
    last(1)
    middle(2)
    gathered(3)
    project(3)
    last(2)
    middle(3)
    last(3)

    sent(KV.at[0:63], skv)
    sent(QS.at[0:P64 - 1], sq)
    sent(MS.at[0:P64 - 1], sm)
    sent(A.at[0:7], sw)
    sent(A.at[0:7], sa)
    sent(PB.at[0:3], sx)
    own_back(0).wait()
    own_back(1).wait()
    sent(o_ref.at[:, 0:14 * 128], so)
    arrived(o_ref.at[:, 0:14 * 128], ro)


WC = 4
EVENTS = (
    "z0 z1 z2 y0 y1 z3 z4 W0 Y0 Q y2",
    "Y1 y3 W1 z5 z6",
    "w10 W2 Y2 y4",
    "z7 w11 W3 Y3 y5",
    "w12 w20 Y4 y6",
    "w13 w21 Y5 y7",
    "w22 w30 Y6",
    "w23 w31 Y7",
    "w32 w33 w40 w41 w42 w43",
)


def layer(q, keys, values, ids, plan, w_out, T=32):
    NT, width = q.shape
    N = 2 * NT + 16
    KD = w_out.shape[0]
    any_ = pl.BlockSpec(memory_space=pl.ANY)
    vm = pl.BlockSpec(memory_space=pltpu.VMEM)
    dma = pltpu.SemaphoreType.DMA
    bf, f32 = jnp.bfloat16, jnp.float32
    B, R, P64 = NT // T, T * (width // HEAD_DIM), NT // 2
    return pl.pallas_call(
        functools.partial(layer_kernel, T, WC, EVENTS),
        out_shape=jax.ShapeDtypeStruct((NT, 16 * 128), bf),
        in_specs=[vm, any_, any_, vm, vm, any_], out_specs=any_,
        scratch_shapes=[
            pltpu.VMEM((64, N, 128), bf), pltpu.VMEM((8, NT, KD), bf), pltpu.VMEM((4, KD, 256), bf),
            pltpu.VMEM((4, 4, 2, 2 * NT, 128), bf), pltpu.VMEM((4, 2, 2 * NT, 128), bf),
            pltpu.VMEM((4, 2, 2, 2 * NT, 128), bf), pltpu.VMEM((4, 2, 2 * NT, 128), bf),
            pltpu.VMEM((B, R, 128), f32), pltpu.VMEM((B, R, 128), f32), pltpu.VMEM((B, R, HEAD_DIM), f32),
            pltpu.VMEM((B, R, 1024), bf),
            pltpu.VMEM((P64 * 16, HEAD_DIM), f32),
            pltpu.VMEM((P64, 16, HEAD_DIM), bf), pltpu.VMEM((P64, 16, HEAD_DIM), bf), pltpu.VMEM((B, R, HEAD_DIM), bf),
            pltpu.VMEM((P64, 1, 128), f32), pltpu.VMEM((P64, 1, 128), f32), pltpu.VMEM((B, T, 256), f32),
            dma, dma, dma, dma, dma, dma((8,)), dma((8,)), dma((8,)), dma((8,)), dma, dma((4, WC)),
            dma, dma((2, 2)), dma, dma((4,)), dma, dma((4, 2)), dma((4, 2)), dma, dma, dma((8,)),
        ],
        compiler_params=pltpu.CompilerParams(collective_id=0, has_side_effects=True, vmem_limit_bytes=48 << 20),
    )(q, keys, values, ids, plan, w_out)


CTX = ("z", "y", "core")


def body(queries, keys, values, doc_ids, plan, w_out):
    return layer(queries, keys, values, doc_ids.reshape(1, -1), plan, w_out)


def solution(mesh):
    fine = Mesh(mesh.devices.reshape(ZN, YN, 2, XN), CTX + ("head",))
    return jax.shard_map(
        body,
        mesh=fine,
        in_specs=(
            P(CTX, "head"),
            P(CTX, "head"),
            P(CTX, "head"),
            P(CTX),
            P(CTX, None),
            P("head", CTX),
        ),
        out_specs=P(CTX, "head"),
        check_vma=False,
    )
```

```python
import functools
import math

import jax
import jax.numpy as jnp
from jax import lax
from jax.experimental import pallas as pl
from jax.experimental.pallas import tpu as pltpu
from jax.sharding import Mesh, PartitionSpec as P

HEAD_DIM = 128
NEG_FILL = -1e30

MESH = pl.DeviceIdType.MESH
STEPS = (0, -1, 1, -2, 2, -3, 3, 4)
ZN, YN, XN = 8, 4, 4


def remote(src, dst, send, recv, **where):
    return pltpu.make_async_remote_copy(
        src_ref=src, dst_ref=dst, send_sem=send, recv_sem=recv,
        device_id=where, device_id_type=MESH)


def layer_kernel(T, WC, plan_a, q_hbm, k_ref, v_ref, id_hbm, plan_hbm, w_ref, o_ref,
                 KV, A, W, PB, RO, RA, FB, M, L, ACC, PR, q_ref, id_ref, plan_ref, QF, QS, QR, Q2, MS, MR, META,
                 sq, rq, sm, rm, skv, rz, ry, ry2, rs, sw, rw,
                 sa, ra, rh, ras, sx, rx, rr, so, ro, lo):
    z, y, k, x = (lax.axis_index(n) for n in ("z", "y", "core", "head"))
    zp, zm = (z + 1) % ZN, (z + ZN - 1) % ZN
    yp, ym, y2 = (y + 1) % YN, (y + YN - 1) % YN, (y + 2) % YN
    xp, xm = (x + 1) % XN, (x + XN - 1) % XN
    sib = 1 - k
    NT = q_hbm.shape[0]
    G = q_hbm.shape[1] // HEAD_DIM
    N = KV.shape[1]
    KD = w_ref.shape[0]
    H, HT, HK = 128, NT // 2, KD // WC
    zs = [(z + d + ZN) % ZN for d in STEPS]
    ys = (y, ym, yp, y2)

    me = (z * YN + y) * 2 + k

    def sent(ref, sem):
        remote(ref, ref, sem, sem, core=1 - k).wait_send()

    def arrived(ref, sem):
        remote(ref, ref, sem, sem, core=1 - k).wait_recv()

    P64 = NT // 2

    barrier = pltpu.get_barrier_semaphore()
    loads = [pltpu.make_async_copy(q_hbm, q_ref, lo.at[0]), pltpu.make_async_copy(id_hbm, id_ref, lo.at[1]),
             pltpu.make_async_copy(plan_hbm, plan_ref, lo.at[2])]
    own_k = pltpu.make_async_copy(k_ref, KV.at[me].at[0:NT], lo.at[3])
    own_v = pltpu.make_async_copy(v_ref, KV.at[me].at[NT:2 * NT], lo.at[4])
    for cp in loads + [own_k, own_v]:
        cp.start()

    def place(d):
        return {"z": d // (2 * YN), "y": (d // 2) % YN, "core": d % 2}

    for to in (xp, xm):
        pl.semaphore_signal(barrier, inc=1, device_id={"head": to}, device_id_type=MESH)

    @pl.loop(1, P64)
    def _(o):
        pl.semaphore_signal(barrier, inc=1, device_id=place((me + o) % P64), device_id_type=MESH)

    group = [(dy, dk) for dy in range(YN) for dk in range(2) if (dy, dk) != (0, 0)]
    for cp in loads:
        cp.wait()
    KV[me, 2 * NT:N, :] = jnp.broadcast_to(id_ref[...].astype(jnp.float32), (16, NT)).astype(jnp.bfloat16)

    row = lax.broadcasted_iota(jnp.int32, (NT, NT), 0)
    lane = lax.broadcasted_iota(jnp.int32, (NT, NT), 1)
    wanted = plan_ref[...] * 2
    wanted = jnp.concatenate([wanted, wanted + 1], axis=1)
    pick = jnp.where(row == wanted, 1.0, 0.0).astype(jnp.bfloat16)
    across = (((0,), (0,)), ((), ()))
    for h in range(G):
        part = lax.dot_general(pick, q_ref[:, h * HEAD_DIM:(h + 1) * HEAD_DIM], across,
                               preferred_element_type=jnp.float32)
        for i in (0, 1):
            QF[pl.ds(2 * h + i, P64, stride=16), :] = part[i * P64:(i + 1) * P64]
    QS[...] = QF[...].astype(jnp.bfloat16).reshape(P64, 16, HEAD_DIM)
    doc = jnp.sum(jnp.where(row == lane, id_ref[...], 0), axis=1, keepdims=True)
    both = 0.0
    for i in (0, 1):
        told = jnp.where(lane == 2 * i, row, jnp.where(lane == 2 * i + 1, doc, 0)).astype(jnp.float32)
        both = both + lax.dot_general(pick[:, i * P64:(i + 1) * P64], told.astype(jnp.bfloat16), across,
                                      preferred_element_type=jnp.float32)
    for j in range(P64):
        MS[j] = both[j:j + 1]

    pl.semaphore_wait(barrier, P64 + 1)

    def slot(zz, yy, kk):
        return KV.at[(zz * YN + yy) * 2 + kk]

    def zc(i, zz, a, b, to, src=None):
        d = slot(zz, y, k).at[a:b]
        return remote(d if src is None else src, d, skv, rz.at[i], z=to)

    z_out = [zc(0, z, 0, N, zp), zc(1, z, 0, N, zm),
             zc(2, zs[1], 0, N, zp), zc(3, zs[2], 0, N, zm),
             zc(4, zs[3], 0, N, zp), zc(5, zs[4], 0, N, zm),
             zc(6, zs[5], 0, H, zp), zc(7, zs[6], H, N, zm)]
    z_in = [zc(0, zs[1], 0, N, zp), zc(1, zs[2], 0, N, zm),
            zc(2, zs[3], 0, N, zp), zc(3, zs[4], 0, N, zm),
            zc(4, zs[5], 0, N, zp), zc(5, zs[6], 0, N, zm),
            zc(6, zs[7], 0, H, zp), zc(7, zs[7], H, N, zm)]

    def yc(s, side, yy, src=None):
        d = slot(zs[s], yy, k)
        return remote(d if src is None else src, d, skv, ry.at[s], y=yp if side == 0 else ym)

    def yc2(s, side, yy):
        d = slot(zs[s], yy, k)
        d = d.at[0:H] if side == 0 else d.at[H:N]
        return remote(d, d, skv, ry2.at[s], y=yp if side == 0 else ym)

    def sc(s, i, kk, src=None):
        d = slot(zs[s], ys[i], kk)
        return remote(d if src is None else src, d, skv, rs.at[s], core=sib)


    def piece(o):
        d = (me + o) % P64
        return (remote(QS.at[d], QR.at[me], sq, rq, **place(d)),
                remote(MS.at[d], MR.at[me], sm, rm, **place(d)))

    own_q = pltpu.make_async_copy(QS.at[me], QR.at[me], lo.at[5])
    own_m = pltpu.make_async_copy(MS.at[me], MR.at[me], lo.at[6])

    def send_queries():
        own_q.start()
        own_m.start()

        @pl.loop(1, P64)
        def _(o):
            for cp in piece(o):
                cp.start()

    def take_queries():
        own_q.wait()
        own_m.wait()

        arrived(QR.at[0:P64 - 1], rq)
        arrived(MR.at[0:P64 - 1], rm)
        QF[...] = QR[...].astype(jnp.float32).reshape(P64 * 16, HEAD_DIM)
        for b in range(B):
            PB_ = T // 2
            q = [QF[pl.ds(b * PB_ * 16 + 2 * h + i, PB_, stride=16), :] for h in range(G) for i in (0, 1)]
            Q2[b] = jnp.concatenate(q, axis=0).astype(jnp.bfloat16)
            told = jnp.concatenate([MR[j] for j in range(b * PB_, (b + 1) * PB_)], axis=0)
            first = ((b * PB_ + lax.broadcasted_iota(jnp.int32, (PB_, 1), 0)) * NT).astype(jnp.float32)
            for i in (0, 1):
                META[b, i * PB_:(i + 1) * PB_, :] = jnp.concatenate(
                    [jnp.broadcast_to(told[:, 2 * i:2 * i + 1] + first, (PB_, 128)),
                     jnp.broadcast_to(told[:, 2 * i + 1:2 * i + 2], (PB_, 128))], axis=1)

    B = NT // T

    def wslot(zz, h):
        return W.at[zz // 2].at[h * HK:(h + 1) * HK, pl.ds(pl.multiple_of((zz % 2) * 128, 128), 128)]

    def wc(dist, side, h, src_z, src=None):
        d = wslot(src_z, h)
        return remote(d if src is None else src, d, sw, rw.at[dist - 1, h], z=zp if side == 0 else zm)

    def zat(side, dist):
        return (z + (ZN - dist if side == 0 else dist)) % ZN

    own_w = pltpu.make_async_copy(
        w_ref, W.at[z // 2].at[:, pl.ds(pl.multiple_of((z % 2) * 128, 128), 128)], lo.at[7])

    def wstart(h):
        for side in (0, 1):
            wc(1, side, h, z, w_ref.at[h * HK:(h + 1) * HK]).start()
        if h == WC - 1:
            own_w.start()

    def wevent(dist, h):
        near = 0 if h < WC // 2 else 1
        if dist == 4:
            arrived(w_ref.at[0:HK], rw.at[3, h])
            return
        arrived(w_ref.at[0:2 * HK], rw.at[dist - 1, h])
        for side in (0, 1):
            if dist < 3 or side == near:
                wc(dist + 1, side, h, zat(side, dist)).start()

    def zstage(s):
        src = None
        if s == 0:
            own_k.wait()
            own_v.wait()
            z_out[0].start()
            z_out[1].start()
        elif s == 7:
            z_in[6].wait_recv()
            z_in[7].wait_recv()
        else:
            z_in[s - 1].wait_recv()
            z_out[s + 1].start()
        yc(s, 0, y, src).start()
        yc(s, 1, y, src).start()
        sc(s, 0, k, src).start()
        if s == 0:
            send_queries()

    def y1stage(s):
        arrived(KV.at[0:2], ry.at[s])
        yc2(s, 0, ym).start()
        yc2(s, 1, yp).start()
        sc(s, 1, k).start()
        sc(s, 2, k).start()

    def y2stage(s):
        arrived(KV.at[0], ry2.at[s])
        sc(s, 3, k).start()

    R = G * T
    TK = 2 * YN * 128
    c = math.log2(math.e) / math.sqrt(HEAD_DIM)
    M[...] = jnp.full_like(M, NEG_FILL)
    L[...] = jnp.zeros_like(L)
    ACC[...] = jnp.zeros_like(ACC)

    per = T * 64 // TK

    def attention(s):
        arrived(KV.at[0:4], rs.at[s])
        away = (s + 1) // 2
        zz = (z + jnp.where(s % 2 == 0, away, ZN - away)) % ZN
        base = zz * 2 * YN

        def against(b0):
            nb = B - b0
            kk = KV[pl.ds(base, 2 * YN), 0:128, :].reshape(TK, HEAD_DIM)
            ids = jnp.concatenate([KV[base + i, 256:272, :].astype(jnp.float32)[0:1] for i in range(2 * YN)], axis=1)
            u = (zz * TK + lax.broadcasted_iota(jnp.int32, (T, TK), 1)).astype(jnp.float32)
            sco = lax.dot_general(Q2[b0:B].reshape(nb * R, HEAD_DIM), kk, (((1,), (1,)), ((), ())),
                                  preferred_element_type=jnp.float32)
            for b in range(b0, B):
                pos, doc = META[b][:, 0:1], META[b][:, 128:129]
                ok = (ids == doc) & (u <= pos)
                sb = sco[(b - b0) * R:(b - b0 + 1) * R].reshape(G, T, TK)
                sb = jnp.where(ok[None], sb, NEG_FILL).reshape(R, TK)
                m = M[b][:, 0:1]
                m_new = jnp.maximum(m, jnp.max(sb, axis=1, keepdims=True))
                p = jnp.exp2((sb - m_new) * c)
                a = jnp.exp2((m - m_new) * c)
                part = p[:, 0:128]
                for i in range(1, TK // 128):
                    part = part + p[:, i * 128:(i + 1) * 128]
                L[b] = L[b] * a + part
                ACC[b] = ACC[b] * a
                M[b] = jnp.broadcast_to(m_new, (R, 128))
                PR[b] = p.astype(jnp.bfloat16)
            vv = KV[pl.ds(base, 2 * YN), 128:256, :].reshape(TK, HEAD_DIM)
            res = jnp.dot(PR[b0:B].reshape(nb * R, TK), vv, preferred_element_type=jnp.float32)
            ACC[b0:B] = ACC[b0:B] + res.reshape(nb, R, HEAD_DIM)

        for b0 in range(B):
            pl.when(zz // per == b0)(functools.partial(against, b0))

    steps = {"z": zstage, "y": y1stage, "Y": y2stage, "Q": take_queries, "W": wstart, "w": wevent}

    def run(events):
        for e in events.split():
            steps[e[0]](*(int(v) for v in e[1:]))

    @pl.loop(0, ZN)
    def _(s):
        for j in range(ZN):
            pl.when(s == j)(functools.partial(run, plan_a[j]))
        attention(s)

    mine = y * 2 + k
    tr, tc = lax.broadcasted_iota(jnp.int32, (T, T), 0), lax.broadcasted_iota(jnp.int32, (T, T), 1)
    order = jnp.where((tr % 2) * (T // 2) + tr // 2 == tc, 1.0, 0.0).astype(jnp.bfloat16)

    @pl.loop(0, B)
    def _(b):
        out = (ACC[b] / jnp.sum(L[b], axis=1, keepdims=True)).astype(jnp.bfloat16)
        rows = pl.ds(pl.multiple_of(b * T, T), T)
        out = jnp.concatenate([out[h * T:(h + 1) * T] for h in range(G)], axis=1)
        A[mine, rows, :] = jnp.dot(order, out, preferred_element_type=jnp.float32).astype(jnp.bfloat16)

    def ac(side, h, yy):
        d = A.at[yy * 2 + k].at[h * HT:(h + 1) * HT]
        return remote(d, d, sa, ra.at[side, h], y=yp if side == 0 else ym)

    def hop(side, yy):
        d = A.at[yy * 2 + k].at[side * HT:(side + 1) * HT]
        return remote(d, d, sa, rh, y=yp if side == 0 else ym)

    def asib(i, kk):
        whole = {0: y, 2: y2}
        if i in whole:
            parts = [A.at[whole[i] * 2 + kk]]
        else:
            h = (i - 1) // 2
            parts = [A.at[ym * 2 + kk].at[h * HT:(h + 1) * HT], A.at[yp * 2 + kk].at[(1 - h) * HT:(2 - h) * HT]]
        for d in parts:
            remote(d, d, sa, ras.at[i], core=sib).start()

    asib(0, k)
    ac(0, 0, y).start()
    ac(1, 1, y).start()
    run(plan_a[ZN])
    own_w.wait()

    R2 = 2 * NT

    def rows_of(r):
        if r in (0, 2):
            return A[pl.ds((y if r == 0 else y2) * 2, 2)].reshape(R2, KD)
        h = (r - 1) // 2
        return jnp.concatenate([A[pl.ds(ym * 2, 2), h * HT:(h + 1) * HT, :].reshape(NT, KD),
                                A[pl.ds(yp * 2, 2), (1 - h) * HT:(2 - h) * HT, :].reshape(NT, KD)], axis=0)

    def compute(r, d):
        res = jnp.dot(rows_of(r), W[(x + d) % XN], preferred_element_type=jnp.float32).astype(jnp.bfloat16)
        for p in (0, 1):
            PB[r, d, p] = res[:, p * 128:(p + 1) * 128]

    def to_adjacent(r, p):
        return remote(PB.at[r, 2, p], RO.at[r, p], sx, rx.at[r, p], head=xp if p == 0 else xm)

    def to_dest(r, side, p):
        return remote(PB.at[r, 1 if side == 0 else 3, p], RA.at[r, side, p], sx, rr.at[r, p],
                      head=xp if side == 0 else xm)

    def project(r):
        compute(r, 2)
        to_adjacent(r, 0).start()
        to_adjacent(r, 1).start()
        compute(r, 1)
        to_dest(r, 0, 1).start()
        compute(r, 3)
        to_dest(r, 1, 0).start()
        compute(r, 0)

    def middle(r):
        for side, p in ((0, 0), (1, 1)):
            to_adjacent(r, p).wait_recv()
            d = 1 if side == 0 else 3
            PB[r, d, p] = (PB[r, d, p].astype(jnp.float32) + RO[r, p].astype(jnp.float32)).astype(jnp.bfloat16)
            to_dest(r, side, p).start()

    def column(p, yy, kk):
        return pl.ds(pl.multiple_of((p * 8 + yy * 2 + kk) * 128, 128), 128)

    def back_to(r, p):
        col = column(p, y, k)
        if r == 0:
            return [remote(FB.at[0, p, pl.ds(pl.multiple_of(sib * NT, NT), NT)], o_ref.at[:, col], so, ro, core=sib)]
        out = []
        for kk in (0, 1):
            if r == 2:
                out.append(remote(FB.at[r, p, kk * NT:(kk + 1) * NT], o_ref.at[:, col], so, ro, y=y2, core=kk))
                continue
            h = (r - 1) // 2
            for n, (yy, hh) in enumerate(((ym, h), (yp, 1 - h))):
                at = n * NT + kk * HT
                out.append(remote(FB.at[r, p, at:at + HT], o_ref.at[hh * HT:(hh + 1) * HT, col], so, ro, y=yy, core=kk))
        return out

    def own_back(p):
        return pltpu.make_async_copy(FB.at[0, p, pl.ds(pl.multiple_of(k * NT, NT), NT)],
                                     o_ref.at[:, column(p, y, k)], lo.at[8 + p])

    def last(r):
        for p in (0, 1):
            arrived(RA.at[r, 0], rr.at[r, p])
            FB[r, p] = (PB[r, 0, p].astype(jnp.float32) + RA[r, 0, p].astype(jnp.float32)
                        + RA[r, 1, p].astype(jnp.float32)).astype(jnp.bfloat16)
            if r == 0:
                own_back(p).start()
            for cp in back_to(r, p):
                cp.start()

    def gathered(i):
        arrived(A.at[0], ras.at[i])

    gathered(0)
    project(0)
    ac(0, 0, ym).wait_recv()
    hop(0, ym).start()
    ac(1, 1, yp).wait_recv()
    hop(1, yp).start()
    asib(1, k)
    ac(0, 1, y).start()
    ac(1, 0, y).start()
    middle(0)
    gathered(1)
    project(1)
    arrived(A.at[0], rh)
    asib(2, k)
    middle(1)
    gathered(2)
    project(2)
    ac(0, 1, ym).wait_recv()
    ac(1, 0, yp).wait_recv()
    asib(3, k)
    last(0)
    gathered(3)
    project(3)
    middle(2)
    last(1)
    middle(3)
    last(2)
    last(3)

    sent(KV.at[0:63], skv)
    sent(QS.at[0:P64 - 1], sq)
    sent(MS.at[0:P64 - 1], sm)
    sent(A.at[0:7], sw)
    sent(A.at[0:7], sa)
    sent(PB.at[0:3], sx)
    own_back(0).wait()
    own_back(1).wait()
    sent(o_ref.at[:, 0:14 * 128], so)
    arrived(o_ref.at[:, 0:14 * 128], ro)


WC = 4
EVENTS = (
    "z0 z1 z2 W0 y0 y1 z3 z4 W1 Y0 Q y2",
    "Y1 y3 z5 z6 W2 w10",
    "Y2 y4 W3 w11 Y3",
    "z7 w12 w20 y5 Y4",
    "w13 w21 y6 Y5",
    "w22 y7 Y6 w30",
    "w23 w31 Y7",
    "w32 w33",
    "w40 w41 w42 w43",
)


def layer(q, keys, values, ids, plan, w_out, T=32):
    NT, width = q.shape
    N = 2 * NT + 16
    KD = w_out.shape[0]
    any_ = pl.BlockSpec(memory_space=pl.ANY)
    dma = pltpu.SemaphoreType.DMA
    bf, f32 = jnp.bfloat16, jnp.float32
    B, R, P64 = NT // T, T * (width // HEAD_DIM), NT // 2
    return pl.pallas_call(
        functools.partial(layer_kernel, T, WC, EVENTS),
        out_shape=jax.ShapeDtypeStruct((NT, 16 * 128), bf),
        in_specs=[any_] * 6, out_specs=any_,
        scratch_shapes=[
            pltpu.VMEM((64, N, 128), bf), pltpu.VMEM((8, NT, KD), bf), pltpu.VMEM((4, KD, 256), bf),
            pltpu.VMEM((4, 4, 2, 2 * NT, 128), bf), pltpu.VMEM((4, 2, 2 * NT, 128), bf),
            pltpu.VMEM((4, 2, 2, 2 * NT, 128), bf), pltpu.VMEM((4, 2, 2 * NT, 128), bf),
            pltpu.VMEM((B, R, 128), f32), pltpu.VMEM((B, R, 128), f32), pltpu.VMEM((B, R, HEAD_DIM), f32),
            pltpu.VMEM((B, R, 1024), bf),
            pltpu.VMEM((NT, width), bf), pltpu.VMEM((1, NT), jnp.int32), pltpu.VMEM((1, P64), jnp.int32),
            pltpu.VMEM((P64 * 16, HEAD_DIM), f32),
            pltpu.VMEM((P64, 16, HEAD_DIM), bf), pltpu.VMEM((P64, 16, HEAD_DIM), bf), pltpu.VMEM((B, R, HEAD_DIM), bf),
            pltpu.VMEM((P64, 1, 128), f32), pltpu.VMEM((P64, 1, 128), f32), pltpu.VMEM((B, T, 256), f32),
            dma, dma, dma, dma, dma, dma((8,)), dma((8,)), dma((8,)), dma((8,)), dma, dma((4, WC)),
            dma, dma((2, 2)), dma, dma((4,)), dma, dma((4, 2)), dma((4, 2)), dma, dma, dma((10,)),
        ],
        compiler_params=pltpu.CompilerParams(collective_id=0, has_side_effects=True, vmem_limit_bytes=60 << 20),
    )(q, keys, values, ids, plan, w_out)


CTX = ("z", "y", "core")


def body(queries, keys, values, doc_ids, plan, w_out):
    return layer(queries, keys, values, doc_ids.reshape(1, -1), plan, w_out)


def solution(mesh):
    fine = Mesh(mesh.devices.reshape(ZN, YN, 2, XN), CTX + ("head",))
    return jax.shard_map(
        body,
        mesh=fine,
        in_specs=(
            P(CTX, "head"),
            P(CTX, "head"),
            P(CTX, "head"),
            P(CTX),
            P(CTX, None),
            P("head", CTX),
        ),
        out_specs=P(CTX, "head"),
        check_vma=False,
    )
```

```python
import functools
import math

import jax
import jax.numpy as jnp
from jax import lax
from jax.experimental import pallas as pl
from jax.experimental.pallas import tpu as pltpu
from jax.sharding import Mesh, PartitionSpec as P

HEAD_DIM = 128
NEG_FILL = -1e30

MESH = pl.DeviceIdType.MESH
STEPS = (0, -1, 1, -2, 2, -3, 3, 4)
ZN, YN, XN = 8, 4, 4


def remote(src, dst, send, recv, **where):
    return pltpu.make_async_remote_copy(
        src_ref=src, dst_ref=dst, send_sem=send, recv_sem=recv,
        device_id=where, device_id_type=MESH)


def layer_kernel(T, WC, plan_a, q_hbm, k_ref, v_ref, id_hbm, plan_hbm, w_ref, o_ref,
                 KV, A, W, PB, RO, RA, FB, M, L, ACC, PR, q_ref, id_ref, plan_ref, QF, QS, QR, Q2, MS, MR, META,
                 sq, rq, sm, rm, skv, rz, ry, ry2, rs, sw, rw,
                 sa, ra, rh, ras, sx, rx, rr, so, ro, lo):
    z, y, k, x = (lax.axis_index(n) for n in ("z", "y", "core", "head"))
    zp, zm = (z + 1) % ZN, (z + ZN - 1) % ZN
    yp, ym, y2 = (y + 1) % YN, (y + YN - 1) % YN, (y + 2) % YN
    xp, xm = (x + 1) % XN, (x + XN - 1) % XN
    sib = 1 - k
    NT = q_hbm.shape[0]
    G = q_hbm.shape[1] // HEAD_DIM
    N = KV.shape[1]
    KD = w_ref.shape[0]
    H, HT, HK = 128, NT // 2, KD // WC
    zs = [(z + d + ZN) % ZN for d in STEPS]
    ys = (y, ym, yp, y2)

    me = (z * YN + y) * 2 + k

    def sent(ref, sem):
        remote(ref, ref, sem, sem, core=1 - k).wait_send()

    def arrived(ref, sem):
        remote(ref, ref, sem, sem, core=1 - k).wait_recv()

    P64 = NT // 2

    barrier = pltpu.get_barrier_semaphore()
    loads = [pltpu.make_async_copy(q_hbm, q_ref, lo.at[0]), pltpu.make_async_copy(id_hbm, id_ref, lo.at[1]),
             pltpu.make_async_copy(plan_hbm, plan_ref, lo.at[2])]
    own_k = pltpu.make_async_copy(k_ref, KV.at[me].at[0:NT], lo.at[3])
    own_v = pltpu.make_async_copy(v_ref, KV.at[me].at[NT:2 * NT], lo.at[4])
    for cp in loads + [own_k, own_v]:
        cp.start()

    def place(d):
        return {"z": d // (2 * YN), "y": (d // 2) % YN, "core": d % 2}

    for to in (xp, xm):
        pl.semaphore_signal(barrier, inc=1, device_id={"head": to}, device_id_type=MESH)

    @pl.loop(1, P64)
    def _(o):
        pl.semaphore_signal(barrier, inc=1, device_id=place((me + o) % P64), device_id_type=MESH)

    group = [(dy, dk) for dy in range(YN) for dk in range(2) if (dy, dk) != (0, 0)]
    for cp in loads:
        cp.wait()
    KV[me, 2 * NT:N, :] = jnp.broadcast_to(id_ref[...].astype(jnp.float32), (16, NT)).astype(jnp.bfloat16)

    row = lax.broadcasted_iota(jnp.int32, (NT, NT), 0)
    lane = lax.broadcasted_iota(jnp.int32, (NT, NT), 1)
    wanted = plan_ref[...] * 2
    wanted = jnp.concatenate([wanted, wanted + 1], axis=1)
    pick = jnp.where(row == wanted, 1.0, 0.0).astype(jnp.bfloat16)
    across = (((0,), (0,)), ((), ()))
    for h in range(G):
        part = lax.dot_general(pick, q_ref[:, h * HEAD_DIM:(h + 1) * HEAD_DIM], across,
                               preferred_element_type=jnp.float32)
        for i in (0, 1):
            QF[pl.ds(2 * h + i, P64, stride=16), :] = part[i * P64:(i + 1) * P64]
    QS[...] = QF[...].astype(jnp.bfloat16).reshape(P64, 16, HEAD_DIM)
    doc = jnp.sum(jnp.where(row == lane, id_ref[...], 0), axis=1, keepdims=True)
    both = 0.0
    for i in (0, 1):
        told = jnp.where(lane == 2 * i, row, jnp.where(lane == 2 * i + 1, doc, 0)).astype(jnp.float32)
        both = both + lax.dot_general(pick[:, i * P64:(i + 1) * P64], told.astype(jnp.bfloat16), across,
                                      preferred_element_type=jnp.float32)
    for j in range(P64):
        MS[j] = both[j:j + 1]

    pl.semaphore_wait(barrier, P64 + 1)

    def slot(zz, yy, kk):
        return KV.at[(zz * YN + yy) * 2 + kk]

    def zc(i, zz, a, b, to, src=None):
        d = slot(zz, y, k).at[a:b]
        return remote(d if src is None else src, d, skv, rz.at[i], z=to)

    z_out = [zc(0, z, 0, N, zp), zc(1, z, 0, N, zm),
             zc(2, zs[1], 0, N, zp), zc(3, zs[2], 0, N, zm),
             zc(4, zs[3], 0, N, zp), zc(5, zs[4], 0, N, zm),
             zc(6, zs[5], 0, H, zp), zc(7, zs[6], H, N, zm)]
    z_in = [zc(0, zs[1], 0, N, zp), zc(1, zs[2], 0, N, zm),
            zc(2, zs[3], 0, N, zp), zc(3, zs[4], 0, N, zm),
            zc(4, zs[5], 0, N, zp), zc(5, zs[6], 0, N, zm),
            zc(6, zs[7], 0, H, zp), zc(7, zs[7], H, N, zm)]

    def yc(s, side, yy, src=None):
        d = slot(zs[s], yy, k)
        return remote(d if src is None else src, d, skv, ry.at[s], y=yp if side == 0 else ym)

    def yc2(s, side, yy):
        d = slot(zs[s], yy, k)
        d = d.at[0:H] if side == 0 else d.at[H:N]
        return remote(d, d, skv, ry2.at[s], y=yp if side == 0 else ym)

    def sc(s, i, kk, src=None):
        d = slot(zs[s], ys[i], kk)
        return remote(d if src is None else src, d, skv, rs.at[s], core=sib)


    def piece(o):
        d = (me + o) % P64
        return (remote(QS.at[d], QR.at[me], sq, rq, **place(d)),
                remote(MS.at[d], MR.at[me], sm, rm, **place(d)))

    own_q = pltpu.make_async_copy(QS.at[me], QR.at[me], lo.at[5])
    own_m = pltpu.make_async_copy(MS.at[me], MR.at[me], lo.at[6])

    def send_queries():
        own_q.start()
        own_m.start()

        @pl.loop(1, P64)
        def _(o):
            for cp in piece(o):
                cp.start()

    def take_queries():
        own_q.wait()
        own_m.wait()

        arrived(QR.at[0:P64 - 1], rq)
        arrived(MR.at[0:P64 - 1], rm)
        QF[...] = QR[...].astype(jnp.float32).reshape(P64 * 16, HEAD_DIM)
        for b in range(B):
            PB_ = T // 2
            q = [QF[pl.ds(b * PB_ * 16 + 2 * h + i, PB_, stride=16), :] for h in range(G) for i in (0, 1)]
            Q2[b] = jnp.concatenate(q, axis=0).astype(jnp.bfloat16)
            told = jnp.concatenate([MR[j] for j in range(b * PB_, (b + 1) * PB_)], axis=0)
            first = ((b * PB_ + lax.broadcasted_iota(jnp.int32, (PB_, 1), 0)) * NT).astype(jnp.float32)
            for i in (0, 1):
                META[b, i * PB_:(i + 1) * PB_, :] = jnp.concatenate(
                    [jnp.broadcast_to(told[:, 2 * i:2 * i + 1] + first, (PB_, 128)),
                     jnp.broadcast_to(told[:, 2 * i + 1:2 * i + 2], (PB_, 128))], axis=1)

    B = NT // T

    def wslot(zz, h):
        return W.at[zz // 2].at[h * HK:(h + 1) * HK, pl.ds(pl.multiple_of((zz % 2) * 128, 128), 128)]

    def wc(dist, side, h, src_z, src=None):
        d = wslot(src_z, h)
        return remote(d if src is None else src, d, sw, rw.at[dist - 1, h], z=zp if side == 0 else zm)

    def zat(side, dist):
        return (z + (ZN - dist if side == 0 else dist)) % ZN

    own_w = pltpu.make_async_copy(
        w_ref, W.at[z // 2].at[:, pl.ds(pl.multiple_of((z % 2) * 128, 128), 128)], lo.at[7])

    def wstart(h):
        for side in (0, 1):
            wc(1, side, h, z, w_ref.at[h * HK:(h + 1) * HK]).start()
        if h == WC - 1:
            own_w.start()

    def wevent(dist, h):
        near = 0 if h < WC // 2 else 1
        if dist == 4:
            arrived(w_ref.at[0:HK], rw.at[3, h])
            return
        arrived(w_ref.at[0:2 * HK], rw.at[dist - 1, h])
        for side in (0, 1):
            if dist < 3 or side == near:
                wc(dist + 1, side, h, zat(side, dist)).start()

    def zstage(s):
        src = None
        if s == 0:
            own_k.wait()
            own_v.wait()
            z_out[0].start()
            z_out[1].start()
        elif s == 7:
            z_in[6].wait_recv()
            z_in[7].wait_recv()
        else:
            z_in[s - 1].wait_recv()
            z_out[s + 1].start()
        yc(s, 0, y, src).start()
        yc(s, 1, y, src).start()
        sc(s, 0, k, src).start()
        if s == 0:
            send_queries()

    def y1stage(s):
        arrived(KV.at[0:2], ry.at[s])
        yc2(s, 0, ym).start()
        yc2(s, 1, yp).start()
        sc(s, 1, k).start()
        sc(s, 2, k).start()

    def y2stage(s):
        arrived(KV.at[0], ry2.at[s])
        sc(s, 3, k).start()

    R = G * T
    TK = 2 * YN * 128
    c = math.log2(math.e) / math.sqrt(HEAD_DIM)
    M[...] = jnp.full_like(M, NEG_FILL)
    L[...] = jnp.zeros_like(L)
    ACC[...] = jnp.zeros_like(ACC)

    per = T * 64 // TK

    def attention(s):
        arrived(KV.at[0:4], rs.at[s])
        away = (s + 1) // 2
        zz = (z + jnp.where(s % 2 == 0, away, ZN - away)) % ZN
        base = zz * 2 * YN

        def against(b0):
            nb = B - b0
            kk = KV[pl.ds(base, 2 * YN), 0:128, :].reshape(TK, HEAD_DIM)
            ids = jnp.concatenate([KV[base + i, 256:272, :].astype(jnp.float32)[0:1] for i in range(2 * YN)], axis=1)
            u = (zz * TK + lax.broadcasted_iota(jnp.int32, (T, TK), 1)).astype(jnp.float32)
            sco = lax.dot_general(Q2[b0:B].reshape(nb * R, HEAD_DIM), kk, (((1,), (1,)), ((), ())),
                                  preferred_element_type=jnp.float32)
            for b in range(b0, B):
                pos, doc = META[b][:, 0:1], META[b][:, 128:129]
                ok = (ids == doc) & (u <= pos)
                sb = sco[(b - b0) * R:(b - b0 + 1) * R].reshape(G, T, TK)
                sb = jnp.where(ok[None], sb, NEG_FILL).reshape(R, TK)
                m = M[b][:, 0:1]
                m_new = jnp.maximum(m, jnp.max(sb, axis=1, keepdims=True))
                p = jnp.exp2((sb - m_new) * c)
                a = jnp.exp2((m - m_new) * c)
                part = p[:, 0:128]
                for i in range(1, TK // 128):
                    part = part + p[:, i * 128:(i + 1) * 128]
                L[b] = L[b] * a + part
                ACC[b] = ACC[b] * a
                M[b] = jnp.broadcast_to(m_new, (R, 128))
                PR[b] = p.astype(jnp.bfloat16)
            vv = KV[pl.ds(base, 2 * YN), 128:256, :].reshape(TK, HEAD_DIM)
            res = jnp.dot(PR[b0:B].reshape(nb * R, TK), vv, preferred_element_type=jnp.float32)
            ACC[b0:B] = ACC[b0:B] + res.reshape(nb, R, HEAD_DIM)

        for b0 in range(B):
            pl.when(zz // per == b0)(functools.partial(against, b0))

    steps = {"z": zstage, "y": y1stage, "Y": y2stage, "Q": take_queries, "W": wstart, "w": wevent}

    def run(events):
        for e in events.split():
            steps[e[0]](*(int(v) for v in e[1:]))

    @pl.loop(0, ZN)
    def _(s):
        for j in range(ZN):
            pl.when(s == j)(functools.partial(run, plan_a[j]))
        attention(s)

    mine = y * 2 + k
    tr, tc = lax.broadcasted_iota(jnp.int32, (T, T), 0), lax.broadcasted_iota(jnp.int32, (T, T), 1)
    order = jnp.where((tr % 2) * (T // 2) + tr // 2 == tc, 1.0, 0.0).astype(jnp.bfloat16)

    @pl.loop(0, B)
    def _(b):
        out = (ACC[b] / jnp.sum(L[b], axis=1, keepdims=True)).astype(jnp.bfloat16)
        rows = pl.ds(pl.multiple_of(b * T, T), T)
        out = jnp.concatenate([out[h * T:(h + 1) * T] for h in range(G)], axis=1)
        A[mine, rows, :] = jnp.dot(order, out, preferred_element_type=jnp.float32).astype(jnp.bfloat16)

    def ac(side, h, yy):
        d = A.at[yy * 2 + k].at[h * HT:(h + 1) * HT]
        return remote(d, d, sa, ra.at[side, h], y=yp if side == 0 else ym)

    def hop(side, yy):
        d = A.at[yy * 2 + k].at[side * HT:(side + 1) * HT]
        return remote(d, d, sa, rh, y=yp if side == 0 else ym)

    def asib(i, kk):
        whole = {0: y, 2: y2}
        if i in whole:
            parts = [A.at[whole[i] * 2 + kk]]
        else:
            h = (i - 1) // 2
            parts = [A.at[ym * 2 + kk].at[h * HT:(h + 1) * HT], A.at[yp * 2 + kk].at[(1 - h) * HT:(2 - h) * HT]]
        for d in parts:
            remote(d, d, sa, ras.at[i], core=sib).start()

    asib(0, k)
    ac(0, 0, y).start()
    ac(1, 1, y).start()
    run(plan_a[ZN])
    own_w.wait()

    R2 = 2 * NT

    def rows_of(r):
        if r in (0, 2):
            return A[pl.ds((y if r == 0 else y2) * 2, 2)].reshape(R2, KD)
        h = (r - 1) // 2
        return jnp.concatenate([A[pl.ds(ym * 2, 2), h * HT:(h + 1) * HT, :].reshape(NT, KD),
                                A[pl.ds(yp * 2, 2), (1 - h) * HT:(2 - h) * HT, :].reshape(NT, KD)], axis=0)

    def compute(r, d):
        res = jnp.dot(rows_of(r), W[(x + d) % XN], preferred_element_type=jnp.float32).astype(jnp.bfloat16)
        for p in (0, 1):
            PB[r, d, p] = res[:, p * 128:(p + 1) * 128]

    def to_adjacent(r, p):
        return remote(PB.at[r, 2, p], RO.at[r, p], sx, rx.at[r, p], head=xp if p == 0 else xm)

    def to_dest(r, side, p):
        return remote(PB.at[r, 1 if side == 0 else 3, p], RA.at[r, side, p], sx, rr.at[r, p],
                      head=xp if side == 0 else xm)

    def project(r, between=None):
        compute(r, 2)
        to_adjacent(r, 0).start()
        to_adjacent(r, 1).start()
        if between is not None:
            between()
        compute(r, 1)
        to_dest(r, 0, 1).start()
        compute(r, 3)
        to_dest(r, 1, 0).start()
        compute(r, 0)

    def middle(r):
        for side, p in ((0, 0), (1, 1)):
            to_adjacent(r, p).wait_recv()
            d = 1 if side == 0 else 3
            PB[r, d, p] = (PB[r, d, p].astype(jnp.float32) + RO[r, p].astype(jnp.float32)).astype(jnp.bfloat16)
            to_dest(r, side, p).start()

    def column(p, yy, kk):
        return pl.ds(pl.multiple_of((p * 8 + yy * 2 + kk) * 128, 128), 128)

    def back_to(r, p):
        col = column(p, y, k)
        if r == 0:
            return [remote(FB.at[0, p, pl.ds(pl.multiple_of(sib * NT, NT), NT)], o_ref.at[:, col], so, ro, core=sib)]
        out = []
        for kk in (0, 1):
            if r == 2:
                out.append(remote(FB.at[r, p, kk * NT:(kk + 1) * NT], o_ref.at[:, col], so, ro, y=y2, core=kk))
                continue
            h = (r - 1) // 2
            for n, (yy, hh) in enumerate(((ym, h), (yp, 1 - h))):
                at = n * NT + kk * HT
                out.append(remote(FB.at[r, p, at:at + HT], o_ref.at[hh * HT:(hh + 1) * HT, col], so, ro, y=yy, core=kk))
        return out

    def own_back(p):
        return pltpu.make_async_copy(FB.at[0, p, pl.ds(pl.multiple_of(k * NT, NT), NT)],
                                     o_ref.at[:, column(p, y, k)], lo.at[8 + p])

    def last(r):
        for p in (0, 1):
            arrived(RA.at[r, 0], rr.at[r, p])
            FB[r, p] = (PB[r, 0, p].astype(jnp.float32) + RA[r, 0, p].astype(jnp.float32)
                        + RA[r, 1, p].astype(jnp.float32)).astype(jnp.bfloat16)
            if r == 0:
                own_back(p).start()
            for cp in back_to(r, p):
                cp.start()

    def gathered(i):
        arrived(A.at[0], ras.at[i])

    gathered(0)
    project(0)
    ac(0, 0, ym).wait_recv()
    hop(0, ym).start()
    ac(1, 1, yp).wait_recv()
    hop(1, yp).start()
    asib(1, k)
    ac(0, 1, y).start()
    ac(1, 0, y).start()
    middle(0)
    gathered(1)
    project(1)
    arrived(A.at[0], rh)
    asib(2, k)
    middle(1)
    gathered(2)
    project(2)
    ac(0, 1, ym).wait_recv()
    ac(1, 0, yp).wait_recv()
    asib(3, k)
    last(0)
    gathered(3)
    project(3, functools.partial(middle, 2))
    last(1)
    middle(3)
    last(2)
    last(3)

    sent(KV.at[0:63], skv)
    sent(QS.at[0:P64 - 1], sq)
    sent(MS.at[0:P64 - 1], sm)
    sent(A.at[0:7], sw)
    sent(A.at[0:7], sa)
    sent(PB.at[0:3], sx)
    own_back(0).wait()
    own_back(1).wait()
    sent(o_ref.at[:, 0:14 * 128], so)
    arrived(o_ref.at[:, 0:14 * 128], ro)


WC = 4
EVENTS = (
    "z0 z1 z2 W0 y0 y1 z3 z4 W1 Y0 Q y2",
    "Y1 y3 z5 z6 W2 w10",
    "Y2 y4 W3 w11 Y3",
    "z7 w12 w20 y5 Y4",
    "w13 w21 y6 Y5",
    "w22 y7 Y6 w30",
    "w23 Y7",
    "w31 w32",
    "w33 w40 w41 w42 w43",
)


def layer(q, keys, values, ids, plan, w_out, T=32):
    NT, width = q.shape
    N = 2 * NT + 16
    KD = w_out.shape[0]
    any_ = pl.BlockSpec(memory_space=pl.ANY)
    dma = pltpu.SemaphoreType.DMA
    bf, f32 = jnp.bfloat16, jnp.float32
    B, R, P64 = NT // T, T * (width // HEAD_DIM), NT // 2
    return pl.pallas_call(
        functools.partial(layer_kernel, T, WC, EVENTS),
        out_shape=jax.ShapeDtypeStruct((NT, 16 * 128), bf),
        in_specs=[any_] * 6, out_specs=any_,
        scratch_shapes=[
            pltpu.VMEM((64, N, 128), bf), pltpu.VMEM((8, NT, KD), bf), pltpu.VMEM((4, KD, 256), bf),
            pltpu.VMEM((4, 4, 2, 2 * NT, 128), bf), pltpu.VMEM((4, 2, 2 * NT, 128), bf),
            pltpu.VMEM((4, 2, 2, 2 * NT, 128), bf), pltpu.VMEM((4, 2, 2 * NT, 128), bf),
            pltpu.VMEM((B, R, 128), f32), pltpu.VMEM((B, R, 128), f32), pltpu.VMEM((B, R, HEAD_DIM), f32),
            pltpu.VMEM((B, R, 1024), bf),
            pltpu.VMEM((NT, width), bf), pltpu.VMEM((1, NT), jnp.int32), pltpu.VMEM((1, P64), jnp.int32),
            pltpu.VMEM((P64 * 16, HEAD_DIM), f32),
            pltpu.VMEM((P64, 16, HEAD_DIM), bf), pltpu.VMEM((P64, 16, HEAD_DIM), bf), pltpu.VMEM((B, R, HEAD_DIM), bf),
            pltpu.VMEM((P64, 1, 128), f32), pltpu.VMEM((P64, 1, 128), f32), pltpu.VMEM((B, T, 256), f32),
            dma, dma, dma, dma, dma, dma((8,)), dma((8,)), dma((8,)), dma((8,)), dma, dma((4, WC)),
            dma, dma((2, 2)), dma, dma((4,)), dma, dma((4, 2)), dma((4, 2)), dma, dma, dma((10,)),
        ],
        compiler_params=pltpu.CompilerParams(collective_id=0, has_side_effects=True, vmem_limit_bytes=60 << 20),
    )(q, keys, values, ids, plan, w_out)


CTX = ("z", "y", "core")


def body(queries, keys, values, doc_ids, plan, w_out):
    return layer(queries, keys, values, doc_ids.reshape(1, -1), plan, w_out)


def solution(mesh):
    fine = Mesh(mesh.devices.reshape(ZN, YN, 2, XN), CTX + ("head",))
    return jax.shard_map(
        body,
        mesh=fine,
        in_specs=(
            P(CTX, "head"),
            P(CTX, "head"),
            P(CTX, "head"),
            P(CTX),
            P(CTX, None),
            P("head", CTX),
        ),
        out_specs=P(CTX, "head"),
        check_vma=False,
    )
```

```python
import functools
import math

import jax
import jax.numpy as jnp
from jax import lax
from jax.experimental import pallas as pl
from jax.experimental.pallas import tpu as pltpu
from jax.sharding import Mesh, PartitionSpec as P

HEAD_DIM = 128
NEG_FILL = -1e30

MESH = pl.DeviceIdType.MESH
STEPS = (0, -1, 1, -2, 2, -3, 3, 4)
ZN, YN, XN = 8, 4, 4


def remote(src, dst, send, recv, **where):
    return pltpu.make_async_remote_copy(
        src_ref=src, dst_ref=dst, send_sem=send, recv_sem=recv,
        device_id=where, device_id_type=MESH)


def layer_kernel(T, WC, plan_a, q_hbm, k_ref, v_ref, id_hbm, plan_hbm, w_ref, o_ref,
                 KV, A, W, PB, RO, RA, FB, M, L, ACC, PR, q_ref, id_ref, plan_ref, QF, QS, QR, Q2, MS, MR, META,
                 sq, rq, sm, rm, skv, rz, ry, ry2, rs, sw, rw,
                 sa, ra, rh, ras, sx, rx, rr, so, ro, lo):
    z, y, k, x = (lax.axis_index(n) for n in ("z", "y", "core", "head"))
    zp, zm = (z + 1) % ZN, (z + ZN - 1) % ZN
    yp, ym, y2 = (y + 1) % YN, (y + YN - 1) % YN, (y + 2) % YN
    xp, xm = (x + 1) % XN, (x + XN - 1) % XN
    sib = 1 - k
    NT = q_hbm.shape[0]
    G = q_hbm.shape[1] // HEAD_DIM
    N = KV.shape[1]
    KD = w_ref.shape[0]
    H, HT, HK = 128, NT // 2, KD // WC
    zs = [(z + d + ZN) % ZN for d in STEPS]
    ys = (y, ym, yp, y2)

    me = (z * YN + y) * 2 + k

    def sent(ref, sem):
        remote(ref, ref, sem, sem, core=1 - k).wait_send()

    def arrived(ref, sem):
        remote(ref, ref, sem, sem, core=1 - k).wait_recv()

    P64 = NT // 2

    barrier = pltpu.get_barrier_semaphore()
    loads = [pltpu.make_async_copy(q_hbm, q_ref, lo.at[0]), pltpu.make_async_copy(id_hbm, id_ref, lo.at[1]),
             pltpu.make_async_copy(plan_hbm, plan_ref, lo.at[2])]
    own_k = pltpu.make_async_copy(k_ref, KV.at[me].at[0:NT], lo.at[3])
    own_v = pltpu.make_async_copy(v_ref, KV.at[me].at[NT:2 * NT], lo.at[4])
    for cp in loads + [own_k, own_v]:
        cp.start()

    def place(d):
        return {"z": d // (2 * YN), "y": (d // 2) % YN, "core": d % 2}

    for to in (xp, xm):
        pl.semaphore_signal(barrier, inc=1, device_id={"head": to}, device_id_type=MESH)

    @pl.loop(1, P64)
    def _(o):
        pl.semaphore_signal(barrier, inc=1, device_id=place((me + o) % P64), device_id_type=MESH)

    group = [(dy, dk) for dy in range(YN) for dk in range(2) if (dy, dk) != (0, 0)]
    for cp in loads:
        cp.wait()
    KV[me, 2 * NT:N, :] = jnp.broadcast_to(id_ref[...].astype(jnp.float32), (16, NT)).astype(jnp.bfloat16)

    row = lax.broadcasted_iota(jnp.int32, (NT, NT), 0)
    lane = lax.broadcasted_iota(jnp.int32, (NT, NT), 1)
    wanted = plan_ref[...] * 2
    wanted = jnp.concatenate([wanted, wanted + 1], axis=1)
    pick = jnp.where(row == wanted, 1.0, 0.0).astype(jnp.bfloat16)
    across = (((0,), (0,)), ((), ()))
    for h in range(G):
        part = lax.dot_general(pick, q_ref[:, h * HEAD_DIM:(h + 1) * HEAD_DIM], across,
                               preferred_element_type=jnp.float32)
        for i in (0, 1):
            QF[pl.ds(2 * h + i, P64, stride=16), :] = part[i * P64:(i + 1) * P64]
    QS[...] = QF[...].astype(jnp.bfloat16).reshape(P64, 16, HEAD_DIM)
    doc = jnp.sum(jnp.where(row == lane, id_ref[...], 0), axis=1, keepdims=True)
    both = 0.0
    for i in (0, 1):
        told = jnp.where(lane == 2 * i, row, jnp.where(lane == 2 * i + 1, doc, 0)).astype(jnp.float32)
        both = both + lax.dot_general(pick[:, i * P64:(i + 1) * P64], told.astype(jnp.bfloat16), across,
                                      preferred_element_type=jnp.float32)
    for j in range(P64):
        MS[j] = both[j:j + 1]

    pl.semaphore_wait(barrier, P64 + 1)

    def slot(zz, yy, kk):
        return KV.at[(zz * YN + yy) * 2 + kk]

    def zc(i, zz, a, b, to, src=None):
        d = slot(zz, y, k).at[a:b]
        return remote(d if src is None else src, d, skv, rz.at[i], z=to)

    z_out = [zc(0, z, 0, N, zp), zc(1, z, 0, N, zm),
             zc(2, zs[1], 0, N, zp), zc(3, zs[2], 0, N, zm),
             zc(4, zs[3], 0, N, zp), zc(5, zs[4], 0, N, zm),
             zc(6, zs[5], 0, H, zp), zc(7, zs[6], H, N, zm)]
    z_in = [zc(0, zs[1], 0, N, zp), zc(1, zs[2], 0, N, zm),
            zc(2, zs[3], 0, N, zp), zc(3, zs[4], 0, N, zm),
            zc(4, zs[5], 0, N, zp), zc(5, zs[6], 0, N, zm),
            zc(6, zs[7], 0, H, zp), zc(7, zs[7], H, N, zm)]

    def yc(s, side, yy, src=None):
        d = slot(zs[s], yy, k)
        return remote(d if src is None else src, d, skv, ry.at[s], y=yp if side == 0 else ym)

    def yc2(s, side, yy):
        d = slot(zs[s], yy, k)
        d = d.at[0:H] if side == 0 else d.at[H:N]
        return remote(d, d, skv, ry2.at[s], y=yp if side == 0 else ym)

    def sc(s, i, kk, src=None):
        d = slot(zs[s], ys[i], kk)
        return remote(d if src is None else src, d, skv, rs.at[s], core=sib)


    def piece(o):
        d = (me + o) % P64
        return (remote(QS.at[d], QR.at[me], sq, rq, **place(d)),
                remote(MS.at[d], MR.at[me], sm, rm, **place(d)))

    own_q = pltpu.make_async_copy(QS.at[me], QR.at[me], lo.at[5])
    own_m = pltpu.make_async_copy(MS.at[me], MR.at[me], lo.at[6])

    def send_queries():
        own_q.start()
        own_m.start()

        @pl.loop(1, P64)
        def _(o):
            for cp in piece(o):
                cp.start()

    def take_queries():
        own_q.wait()
        own_m.wait()

        arrived(QR.at[0:P64 - 1], rq)
        arrived(MR.at[0:P64 - 1], rm)
        QF[...] = QR[...].astype(jnp.float32).reshape(P64 * 16, HEAD_DIM)
        for b in range(B):
            PB_ = T // 2
            q = [QF[pl.ds(b * PB_ * 16 + 2 * h + i, PB_, stride=16), :] for h in range(G) for i in (0, 1)]
            Q2[b] = jnp.concatenate(q, axis=0).astype(jnp.bfloat16)
            told = jnp.concatenate([MR[j] for j in range(b * PB_, (b + 1) * PB_)], axis=0)
            first = ((b * PB_ + lax.broadcasted_iota(jnp.int32, (PB_, 1), 0)) * NT).astype(jnp.float32)
            for i in (0, 1):
                META[b, i * PB_:(i + 1) * PB_, :] = jnp.concatenate(
                    [jnp.broadcast_to(told[:, 2 * i:2 * i + 1] + first, (PB_, 128)),
                     jnp.broadcast_to(told[:, 2 * i + 1:2 * i + 2], (PB_, 128))], axis=1)

    B = NT // T

    def wslot(zz, h):
        return W.at[zz // 2].at[h * HK:(h + 1) * HK, pl.ds(pl.multiple_of((zz % 2) * 128, 128), 128)]

    def wc(dist, side, h, src_z, src=None):
        d = wslot(src_z, h)
        return remote(d if src is None else src, d, sw, rw.at[dist - 1, h], z=zp if side == 0 else zm)

    def zat(side, dist):
        return (z + (ZN - dist if side == 0 else dist)) % ZN

    own_w = pltpu.make_async_copy(
        w_ref, W.at[z // 2].at[:, pl.ds(pl.multiple_of((z % 2) * 128, 128), 128)], lo.at[7])

    def wstart(h):
        for side in (0, 1):
            wc(1, side, h, z, w_ref.at[h * HK:(h + 1) * HK]).start()
        if h == WC - 1:
            own_w.start()

    def wevent(dist, h):
        near = 0 if h < WC // 2 else 1
        if dist == 4:
            arrived(w_ref.at[0:HK], rw.at[3, h])
            return
        arrived(w_ref.at[0:2 * HK], rw.at[dist - 1, h])
        for side in (0, 1):
            if dist < 3 or side == near:
                wc(dist + 1, side, h, zat(side, dist)).start()

    def zstage(s):
        src = None
        if s == 0:
            own_k.wait()
            own_v.wait()
            z_out[0].start()
            z_out[1].start()
        elif s == 7:
            z_in[6].wait_recv()
            z_in[7].wait_recv()
        else:
            z_in[s - 1].wait_recv()
            z_out[s + 1].start()
        yc(s, 0, y, src).start()
        yc(s, 1, y, src).start()
        sc(s, 0, k, src).start()
        if s == 0:
            send_queries()

    def y1stage(s):
        arrived(KV.at[0:2], ry.at[s])
        yc2(s, 0, ym).start()
        yc2(s, 1, yp).start()
        sc(s, 1, k).start()
        sc(s, 2, k).start()

    def y2stage(s):
        arrived(KV.at[0], ry2.at[s])
        sc(s, 3, k).start()

    R = G * T
    TK = 2 * YN * 128
    c = math.log2(math.e) / math.sqrt(HEAD_DIM)
    M[...] = jnp.full_like(M, NEG_FILL)
    L[...] = jnp.zeros_like(L)
    ACC[...] = jnp.zeros_like(ACC)

    per = T * 64 // TK

    def attention(s):
        arrived(KV.at[0:4], rs.at[s])
        away = (s + 1) // 2
        zz = (z + jnp.where(s % 2 == 0, away, ZN - away)) % ZN
        base = zz * 2 * YN

        def against(b0):
            nb = B - b0
            kk = KV[pl.ds(base, 2 * YN), 0:128, :].reshape(TK, HEAD_DIM)
            ids = jnp.concatenate([KV[base + i, 256:272, :].astype(jnp.float32)[0:1] for i in range(2 * YN)], axis=1)
            u = (zz * TK + lax.broadcasted_iota(jnp.int32, (T, TK), 1)).astype(jnp.float32)
            sco = lax.dot_general(Q2[b0:B].reshape(nb * R, HEAD_DIM), kk, (((1,), (1,)), ((), ())),
                                  preferred_element_type=jnp.float32)
            for b in range(b0, B):
                pos, doc = META[b][:, 0:1], META[b][:, 128:129]
                ok = (ids == doc) & (u <= pos)
                sb = sco[(b - b0) * R:(b - b0 + 1) * R].reshape(G, T, TK)
                sb = jnp.where(ok[None], sb, NEG_FILL).reshape(R, TK)
                m = M[b][:, 0:1]
                m_new = jnp.maximum(m, jnp.max(sb, axis=1, keepdims=True))
                p = jnp.exp2((sb - m_new) * c)
                a = jnp.exp2((m - m_new) * c)
                part = p[:, 0:128]
                for i in range(1, TK // 128):
                    part = part + p[:, i * 128:(i + 1) * 128]
                L[b] = L[b] * a + part
                ACC[b] = ACC[b] * a
                M[b] = jnp.broadcast_to(m_new, (R, 128))
                PR[b] = p.astype(jnp.bfloat16)
            vv = KV[pl.ds(base, 2 * YN), 128:256, :].reshape(TK, HEAD_DIM)
            res = jnp.dot(PR[b0:B].reshape(nb * R, TK), vv, preferred_element_type=jnp.float32)
            ACC[b0:B] = ACC[b0:B] + res.reshape(nb, R, HEAD_DIM)

        for b0 in range(B):
            pl.when(zz // per == b0)(functools.partial(against, b0))

    steps = {"z": zstage, "y": y1stage, "Y": y2stage, "Q": take_queries, "W": wstart, "w": wevent}

    def run(events):
        for e in events:
            steps[e[0]](*(int(v) for v in e[1:]))

    @pl.loop(0, ZN)
    def _(s):
        for j in range(ZN):
            pl.when(s == j)(functools.partial(run, plan_a[j]))
        attention(s)

    mine = y * 2 + k
    tr, tc = lax.broadcasted_iota(jnp.int32, (T, T), 0), lax.broadcasted_iota(jnp.int32, (T, T), 1)
    order = jnp.where((tr % 2) * (T // 2) + tr // 2 == tc, 1.0, 0.0).astype(jnp.bfloat16)

    @pl.loop(0, B)
    def _(b):
        out = (ACC[b] / jnp.sum(L[b], axis=1, keepdims=True)).astype(jnp.bfloat16)
        rows = pl.ds(pl.multiple_of(b * T, T), T)
        out = jnp.concatenate([out[h * T:(h + 1) * T] for h in range(G)], axis=1)
        A[mine, rows, :] = jnp.dot(order, out, preferred_element_type=jnp.float32).astype(jnp.bfloat16)

    def ac(side, h, yy):
        d = A.at[yy * 2 + k].at[h * HT:(h + 1) * HT]
        return remote(d, d, sa, ra.at[side, h], y=yp if side == 0 else ym)

    def hop(side, yy):
        d = A.at[yy * 2 + k].at[side * HT:(side + 1) * HT]
        return remote(d, d, sa, rh, y=yp if side == 0 else ym)

    def asib(i, kk):
        whole = {0: y, 2: y2}
        if i in whole:
            parts = [A.at[whole[i] * 2 + kk]]
        else:
            h = (i - 1) // 2
            parts = [A.at[ym * 2 + kk].at[h * HT:(h + 1) * HT], A.at[yp * 2 + kk].at[(1 - h) * HT:(2 - h) * HT]]
        for d in parts:
            remote(d, d, sa, ras.at[i], core=sib).start()

    asib(0, k)
    ac(0, 0, y).start()
    ac(1, 1, y).start()
    run(plan_a[ZN])
    own_w.wait()

    R2 = 2 * NT

    def rows_of(r):
        if r in (0, 2):
            return A[pl.ds((y if r == 0 else y2) * 2, 2)].reshape(R2, KD)
        h = (r - 1) // 2
        return jnp.concatenate([A[pl.ds(ym * 2, 2), h * HT:(h + 1) * HT, :].reshape(NT, KD),
                                A[pl.ds(yp * 2, 2), (1 - h) * HT:(2 - h) * HT, :].reshape(NT, KD)], axis=0)

    def compute(r, d):
        res = jnp.dot(rows_of(r), W[(x + d) % XN], preferred_element_type=jnp.float32).astype(jnp.bfloat16)
        for p in (0, 1):
            PB[r, d, p] = res[:, p * 128:(p + 1) * 128]

    def to_adjacent(r, p):
        return remote(PB.at[r, 2, p], RO.at[r, p], sx, rx.at[r, p], head=xp if p == 0 else xm)

    def to_dest(r, side, p):
        return remote(PB.at[r, 1 if side == 0 else 3, p], RA.at[r, side, p], sx, rr.at[r, p],
                      head=xp if side == 0 else xm)

    def project(r, between=None):
        compute(r, 2)
        to_adjacent(r, 0).start()
        to_adjacent(r, 1).start()
        if between is not None:
            between()
        compute(r, 1)
        to_dest(r, 0, 1).start()
        compute(r, 3)
        to_dest(r, 1, 0).start()
        compute(r, 0)

    def middle(r):
        for side, p in ((0, 0), (1, 1)):
            to_adjacent(r, p).wait_recv()
            d = 1 if side == 0 else 3
            PB[r, d, p] = (PB[r, d, p].astype(jnp.float32) + RO[r, p].astype(jnp.float32)).astype(jnp.bfloat16)
            to_dest(r, side, p).start()

    def column(p, yy, kk):
        return pl.ds(pl.multiple_of((p * 8 + yy * 2 + kk) * 128, 128), 128)

    def back_to(r, p):
        col = column(p, y, k)
        if r == 0:
            return [remote(FB.at[0, p, pl.ds(pl.multiple_of(sib * NT, NT), NT)], o_ref.at[:, col], so, ro, core=sib)]
        out = []
        for kk in (0, 1):
            if r == 2:
                out.append(remote(FB.at[r, p, kk * NT:(kk + 1) * NT], o_ref.at[:, col], so, ro, y=y2, core=kk))
                continue
            h = (r - 1) // 2
            for n, (yy, hh) in enumerate(((ym, h), (yp, 1 - h))):
                at = n * NT + kk * HT
                out.append(remote(FB.at[r, p, at:at + HT], o_ref.at[hh * HT:(hh + 1) * HT, col], so, ro, y=yy, core=kk))
        return out

    def own_back(p):
        return pltpu.make_async_copy(FB.at[0, p, pl.ds(pl.multiple_of(k * NT, NT), NT)],
                                     o_ref.at[:, column(p, y, k)], lo.at[8 + p])

    def last(r):
        for p in (0, 1):
            arrived(RA.at[r, 0], rr.at[r, p])
            FB[r, p] = (PB[r, 0, p].astype(jnp.float32) + RA[r, 0, p].astype(jnp.float32)
                        + RA[r, 1, p].astype(jnp.float32)).astype(jnp.bfloat16)
            if r == 0:
                own_back(p).start()
            for cp in back_to(r, p):
                cp.start()

    def gathered(i):
        arrived(A.at[0], ras.at[i])

    gathered(0)
    project(0)
    ac(0, 0, ym).wait_recv()
    hop(0, ym).start()
    ac(1, 1, yp).wait_recv()
    hop(1, yp).start()
    asib(1, k)
    ac(0, 1, y).start()
    ac(1, 0, y).start()
    middle(0)
    gathered(1)
    project(1)
    arrived(A.at[0], rh)
    asib(2, k)
    middle(1)
    gathered(2)
    project(2)
    ac(0, 1, ym).wait_recv()
    ac(1, 0, yp).wait_recv()
    asib(3, k)
    last(0)
    gathered(3)
    project(3, functools.partial(middle, 2))
    last(1)
    middle(3)
    last(2)
    last(3)

    sent(KV.at[0:63], skv)
    sent(QS.at[0:P64 - 1], sq)
    sent(MS.at[0:P64 - 1], sm)
    sent(A.at[0:7], sw)
    sent(A.at[0:7], sa)
    sent(PB.at[0:3], sx)
    own_back(0).wait()
    own_back(1).wait()
    sent(o_ref.at[:, 0:14 * 128], so)
    arrived(o_ref.at[:, 0:14 * 128], ro)


WC = 4
EVENTS = (
    ("z0", "z1", "z2", "W0", "y0", "y1", "z3", "z4", "W1", "Y0", "Q", "y2",),
    ("Y1", "y3", "z5", "z6", "W2", "w10",),
    ("Y2", "y4", "W3", "w11", "Y3",),
    ("z7", "w12", "w20", "y5", "Y4",),
    ("w13", "w21", "y6", "Y5",),
    ("w22", "y7", "Y6", "w30",),
    ("w23", "Y7",),
    ("w31", "w32",),
    ("w33", "w40", "w41", "w42", "w43",),
)


def layer(q, keys, values, ids, plan, w_out, T=32):
    NT, width = q.shape
    N = 2 * NT + 16
    KD = w_out.shape[0]
    any_ = pl.BlockSpec(memory_space=pl.ANY)
    dma = pltpu.SemaphoreType.DMA
    bf, f32 = jnp.bfloat16, jnp.float32
    B, R, P64 = NT // T, T * (width // HEAD_DIM), NT // 2
    return pl.pallas_call(
        functools.partial(layer_kernel, T, WC, EVENTS),
        out_shape=jax.ShapeDtypeStruct((NT, 16 * 128), bf),
        in_specs=[any_] * 6, out_specs=any_,
        scratch_shapes=[
            pltpu.VMEM((64, N, 128), bf), pltpu.VMEM((8, NT, KD), bf), pltpu.VMEM((4, KD, 256), bf),
            pltpu.VMEM((4, 4, 2, 2 * NT, 128), bf), pltpu.VMEM((4, 2, 2 * NT, 128), bf),
            pltpu.VMEM((4, 2, 2, 2 * NT, 128), bf), pltpu.VMEM((4, 2, 2 * NT, 128), bf),
            pltpu.VMEM((B, R, 128), f32), pltpu.VMEM((B, R, 128), f32), pltpu.VMEM((B, R, HEAD_DIM), f32),
            pltpu.VMEM((B, R, 1024), bf),
            pltpu.VMEM((NT, width), bf), pltpu.VMEM((1, NT), jnp.int32), pltpu.VMEM((1, P64), jnp.int32),
            pltpu.VMEM((P64 * 16, HEAD_DIM), f32),
            pltpu.VMEM((P64, 16, HEAD_DIM), bf), pltpu.VMEM((P64, 16, HEAD_DIM), bf), pltpu.VMEM((B, R, HEAD_DIM), bf),
            pltpu.VMEM((P64, 1, 128), f32), pltpu.VMEM((P64, 1, 128), f32), pltpu.VMEM((B, T, 256), f32),
            dma, dma, dma, dma, dma, dma((8,)), dma((8,)), dma((8,)), dma((8,)), dma, dma((4, WC)),
            dma, dma((2, 2)), dma, dma((4,)), dma, dma((4, 2)), dma((4, 2)), dma, dma, dma((10,)),
        ],
        compiler_params=pltpu.CompilerParams(collective_id=0, has_side_effects=True, vmem_limit_bytes=60 << 20),
    )(q, keys, values, ids, plan, w_out)


CTX = ("z", "y", "core")


def body(queries, keys, values, doc_ids, plan, w_out):
    return layer(queries, keys, values, doc_ids.reshape(1, -1), plan, w_out)


def solution(mesh):
    fine = Mesh(mesh.devices.reshape(ZN, YN, 2, XN), CTX + ("head",))
    return jax.shard_map(
        body,
        mesh=fine,
        in_specs=(
            P(CTX, "head"),
            P(CTX, "head"),
            P(CTX, "head"),
            P(CTX),
            P(CTX, None),
            P("head", CTX),
        ),
        out_specs=P(CTX, "head"),
        check_vma=False,
    )
```
